256 devices in a mesh: rep: 16 (over x, z_hi), tp: 16 (over y, z_lo, core).
Axes of the slice: x: 4, y: 4, z: 8 (z_hi: 4, z_lo: 2; z = z_hi * 2 + z_lo), core: 2. Of those that a mesh axis runs over, the one named last changes fastest.
Arguments:
- hidden: bfloat16 [8192, 8192], P(('rep', 'tp')), may hold values from -6 to 6
- norm_gain: bfloat16 [8192], replicated, may hold values from 0.099609375 to 1.8984375
- q_weight: bfloat16 [8192, 8192], P('rep', 'tp')
- kv_weight: bfloat16 [8192, 2048], P('rep'), may hold values from -0.0625 to 0.0625
- out_weight: bfloat16 [8192, 8192], P('tp', 'rep'), may hold values from -0.0625 to 0.0625
- held_slice: int32 [16], replicated, may hold values from 0 to 15, each once
Outputs:
- attended: bfloat16 [8192, 8192], P(('rep', 'tp'))
The draws below stay inside these ranges and needn't reach their ends.
Inputs may be any that keep to these rules, and one draw needn't show every extreme that they name: `held_slice`: each slice number appears once.
All inputs are finite; a program needn't handle non-finite values.
Results may differ from the reference program's by a relative error of at most 0.019.
The reference program's roundings to bfloat16 on the way count: a program that leaves them out, or rounds other values in their place, can miss the bound.
Values may be sent and summed in bfloat16 or wider, within the bound.
A program may use at most 128 MiB of HBM per device.

```python
import jax
import jax.numpy as jnp
from jax import lax

D = 8192
HD = 128
HQ = 64
KVH = 8
SEQ = 512
TOKENS = 8192
N_REP = 16
N_TP = 16


def draw_q_weight(key, part):
    first = jax.random.fold_in(jax.random.fold_in(key, 17), 0)
    base = jax.random.truncated_normal(first, -4.0, 4.0, (D, HQ * HD), jnp.float32) * D ** (-0.5)
    return base.astype(jnp.bfloat16)


def levels(rng, dims, cuts, low, largest):
    gain, own = 1.0, jax.random.fold_in(rng, 6)
    for position, shards_of in cuts:
        draws = jnp.exp(jax.random.uniform(jax.random.fold_in(own, position), (shards_of,), jnp.float32, low / len(cuts), largest / len(cuts)))
        gain = gain * jnp.repeat(draws, dims[position] // shards_of).reshape([-1 if axis == position else 1 for axis in range(len(dims))])
    return gain


def noise(stream_key, extent, deviation, bound, cuts=(), kind=jnp.bfloat16):
    gain = levels(stream_key, extent, cuts, -0.22, 0.18) if cuts else 1.0
    result = jax.random.normal(stream_key, extent, jnp.float32) * deviation * gain
    return jnp.minimum(jnp.maximum(result, -bound), bound).astype(kind)


def setup_inputs(seed: int = 0) -> dict:
    key_list = jax.random.split(jax.random.key(seed), 7)
    hidden = noise(key_list[0], (TOKENS, D), 1.0, 6.0, ((0, 256),))
    norm_gain = jnp.clip(1.0 + 0.18 * jax.random.normal(key_list[1], (D,), jnp.float32), 0.099609375, 1.8984375).astype(jnp.bfloat16)
    q_weight = draw_q_weight(jax.random.fold_in(key_list[6], 71), 0)
    kv_weight = noise(key_list[3], (D, 2 * KVH * HD), D ** -0.5, 0.0625, ((0, 16),))
    out_weight = noise(key_list[4], (HQ * HD, D), (HQ * HD) ** -0.5, 0.0625, ((0, 16), (1, 16)))
    held_slice = jax.random.permutation(key_list[5], N_REP).astype(jnp.int32)
    return dict(hidden=hidden, norm_gain=norm_gain, q_weight=q_weight, kv_weight=kv_weight, out_weight=out_weight, held_slice=held_slice)


rope_theta = 500000.0

def rotate(states, positions):
    half = states.shape[-1] // 2
    freqs = rope_theta ** (-(jnp.arange(half, dtype=jnp.float32) * 2.0) / states.shape[-1])
    angles = positions[:, None] * freqs[None, :]
    cosine = jnp.cos(angles)[:, None, :]
    sine = jnp.sin(angles)[:, None, :]
    first = states[..., :half]
    second = states[..., half:]
    return jnp.concatenate([first * cosine - second * sine, second * cosine + first * sine], axis=-1)

def reference(hidden, norm_gain, q_weight, kv_weight, out_weight, held_slice):
    parts = N_REP
    slice_rows = D // parts
    inverse = jnp.zeros((parts,), jnp.int32).at[held_slice].set(jnp.arange(parts, dtype=jnp.int32))
    query_full = q_weight.reshape(parts, slice_rows, HQ * HD)[inverse].reshape(D, HQ * HD)
    pair_full = kv_weight.reshape(parts, slice_rows, 2 * KVH * HD)[inverse].reshape(D, 2 * KVH * HD)
    out_full = out_weight.reshape(HQ * HD, parts, slice_rows)[:, inverse, :].reshape(HQ * HD, D)
    prompts = hidden.reshape(N_REP, SEQ, D)
    positions = jnp.arange(SEQ, dtype=jnp.int32)
    group_size = HQ // KVH
    scale = 1.0 / HD ** 0.5

    def one_instance(prompt):
        states = prompt.astype(jnp.float32)
        meansq = lax.optimization_barrier(jnp.mean(states * states, axis=-1, keepdims=True))
        normed = (states * lax.rsqrt(meansq + 1e-05) * norm_gain.astype(jnp.float32)).astype(jnp.bfloat16)
        queries = jnp.dot(normed, query_full, preferred_element_type=jnp.float32).reshape(SEQ, HQ, HD)
        pairs = jnp.dot(normed, pair_full, preferred_element_type=jnp.float32)
        keys = pairs[:, :KVH * HD].reshape(SEQ, KVH, HD)
        values = pairs[:, KVH * HD:].reshape(SEQ, KVH, HD).astype(jnp.bfloat16)
        where_at = positions.astype(jnp.float32)
        queries = rotate(queries, where_at).astype(jnp.bfloat16)
        keys = rotate(keys, where_at).astype(jnp.bfloat16)
        keys_wide = jnp.repeat(keys, group_size, axis=1)
        values_wide = jnp.repeat(values, group_size, axis=1)
        scores = jnp.einsum('shd,thd->hst', queries.astype(jnp.float32), keys_wide.astype(jnp.float32)) * scale
        allowed = positions[:, None] >= positions[None, :]
        scores = jnp.where(allowed[None, :, :], scores, -1e+30)
        peak = lax.optimization_barrier(jnp.max(scores, axis=-1, keepdims=True))
        weights = jnp.exp(scores - peak)
        probs = (weights / lax.optimization_barrier(jnp.sum(weights, axis=-1, keepdims=True))).astype(jnp.bfloat16)
        context = jnp.einsum('hst,thd->shd', probs.astype(jnp.float32), values_wide.astype(jnp.float32))
        context = context.astype(jnp.bfloat16).reshape(SEQ, HQ * HD)
        group_cols = HQ * HD // N_TP
        partial_value = jnp.einsum('snc,ncd->nsd', context.reshape(SEQ, N_TP, group_cols).astype(jnp.float32), out_full.reshape(N_TP, group_cols, D).astype(jnp.float32))
        partial_value = partial_value.astype(jnp.bfloat16).astype(jnp.float32)
        return lax.optimization_barrier(jnp.sum(partial_value, axis=0)).astype(jnp.bfloat16)
    return lax.map(one_instance, prompts).reshape(N_REP * SEQ, D)
```

```python
import functools

import jax
import jax.numpy as jnp
import numpy as np
from jax import lax
from jax.experimental import pallas as pl
from jax.experimental.pallas import tpu as pltpu
from jax.sharding import PartitionSpec as P

HD = 128
HQ = 64
KVH = 8
D = 8192
SEQ = 512
SL = 512
WC = 640
ROPE_THETA = 500000.0
MESH = pl.DeviceIdType.MESH
F32, BF16 = jnp.float32, jnp.bfloat16

CORE = (0, 0, 0, 0, 1)
ZL = (0, 0, 0, 1, 0)
PLANE = [(0, dy, 0, dz, 0) for dy in (1, 3, 2, 0) for dz in (0, 1) if (dy, dz) != (0, 0)]


def x_by(d):
    return (d % 4, 0, 0, 0, 0)


def z_by(d):
    return (0, 0, d % 4, 0, 0)


def y_by(d):
    return (0, d % 4, 0, 0, 0)


PEERS = [x_by(1), x_by(2), x_by(3), z_by(1), z_by(3), CORE] + PLANE


def kernel(held, slots, hidden, gain, q_weight, kv_weight, out_weight, cos_hbm, sin_hbm, out,
           hid, gn, cos, sin, tok, w, wo, acc, kv, q, ctx, give, got, ss, red, fin, parts, lsem, ssem, rsem):
    rep, tp = lax.axis_index("rep"), lax.axis_index("tp")
    x, zh = rep // 4, rep % 4
    y, zl, c = tp // 4, (tp // 2) % 2, tp % 2

    def target(rel):
        dx, dy, dz, dl, dc = rel
        return (
            (x + dx) % 4 * 4 + (zh + dz) % 4,
            (y + dy) % 4 * 4 + (zl + dl) % 2 * 2 + (c + dc) % 2,
        )

    copies = []

    def send(src, dst, rel):
        k = len(copies)
        copy = pltpu.make_async_remote_copy(
            src_ref=src, dst_ref=dst, send_sem=ssem.at[k], recv_sem=rsem.at[k],
            device_id=target(rel), device_id_type=MESH)
        copy.start()
        copies.append(copy)
        return copy

    group = y * 2 + zl
    locals_ = [
        pltpu.make_async_copy(q_weight, w.at[0, :, pl.ds(0, SL)], lsem.at[0]),
        pltpu.make_async_copy(
            kv_weight.at[:, pl.ds(pl.multiple_of(c * KVH * HD + group * HD, HD), HD)],
            w.at[0, :, pl.ds(SL, HD)], lsem.at[1]),
        pltpu.make_async_copy(hidden, hid, lsem.at[2]),
        pltpu.make_async_copy(gain, gn, lsem.at[3]),
        pltpu.make_async_copy(out_weight, wo.at[0], lsem.at[4]),
        pltpu.make_async_copy(cos_hbm, cos, lsem.at[5]),
        pltpu.make_async_copy(sin_hbm, sin, lsem.at[6]),
    ]
    for copy in locals_:
        copy.start()

    barrier = pltpu.get_barrier_semaphore()
    for rel in PEERS:
        pl.semaphore_signal(barrier, inc=1, device_id=target(rel), device_id_type=MESH)
    pl.semaphore_wait(barrier, len(PEERS))

    def full(dx, dz):
        return w.at[dx % 4 * 4 + dz % 4]

    def half(dx, dz, part):
        return w.at[dx % 4 * 4 + dz % 4, pl.ds(part * (SL // 2), SL // 2), :]

    def x_send(dz):
        return send(full(0, dz), full(-1, dz), x_by(1)), send(full(0, dz), full(1, dz), x_by(-1))

    def x_forward(pair, dz):
        pair[0].wait_recv()
        a = send(half(-1, dz, 0), half(-2, dz, 0), x_by(1))
        pair[1].wait_recv()
        b = send(half(1, dz, 1), half(2, dz, 1), x_by(-1))
        return a, b

    locals_[0].wait()
    locals_[1].wait()
    z_pair = send(full(0, 0), full(0, -1), z_by(1)), send(full(0, 0), full(0, 1), z_by(-1))
    x0 = x_send(0)

    def rows(dy, dl, dc=0):
        return pl.ds(pl.multiple_of((c + dc) % 2 * 256 + ((y + dy) % 4 * 2 + (zl + dl) % 2) * 32, 32), 32)

    locals_[2].wait()
    locals_[3].wait()
    states = hid[...].astype(F32)
    meansq = jnp.mean(states * states, axis=-1, keepdims=True)
    scaled = (states * lax.rsqrt(meansq + 1e-05) * gn[...].astype(F32)).astype(BF16)
    for n in range(16):
        tok[n, rows(0, 0), :] = scaled[:, n * SL:(n + 1) * SL]

    def tok_at(dy, dl):
        return tok.at[:, rows(dy, dl), :]

    t_z = send(tok_at(0, 0), tok_at(0, 0), ZL)
    t_y0 = [send(tok_at(0, 0), tok_at(0, 0), y_by(d)) for d in (1, 3, 2)]
    t_core = [send(tok_at(0, 0), tok_at(0, 0), CORE)]
    t_z.wait_recv()
    t_y1 = [send(tok_at(0, 1), tok_at(0, 1), y_by(d)) for d in (1, 3, 2)]
    t_core.append(send(tok_at(0, 1), tok_at(0, 1), CORE))

    h0 = x_forward(x0, 0)
    z_pair[0].wait_recv()
    zf0 = send(half(0, -1, 0), half(0, -2, 0), z_by(1))
    x3 = x_send(-1)
    z_pair[1].wait_recv()
    zf1 = send(half(0, 1, 1), half(0, 2, 1), z_by(-1))
    x1 = x_send(1)
    locals_[4].wait()
    wo_pair = send(wo.at[0], wo.at[3], z_by(1)), send(wo.at[0], wo.at[1], z_by(-1))
    for d, copy in zip((1, 3, 2), t_y0):
        copy.wait_recv()
        t_core.append(send(tok_at(-d, 0), tok_at(-d, 0), CORE))
    zf0.wait_recv()
    zf1.wait_recv()
    x2 = x_send(2)
    h3 = x_forward(x3, -1)
    for d, copy in zip((1, 3, 2), t_y1):
        copy.wait_recv()
        t_core.append(send(tok_at(-d, 1), tok_at(-d, 1), CORE))
    h1 = x_forward(x1, 1)
    wo_pair[0].wait_recv()
    wf0 = send(wo.at[3, pl.ds(0, 256), :], wo.at[2, pl.ds(0, 256), :], z_by(1))
    wo_pair[1].wait_recv()
    wf1 = send(wo.at[1, pl.ds(256, 256), :], wo.at[2, pl.ds(256, 256), :], z_by(-1))
    for copy in t_core:
        copy.wait_recv()

    acc[...] = jnp.zeros_like(acc)

    def project(dx, dz):
        source = held[(x + dx) % 4 * 4 + (zh + dz) % 4]
        slot = dx % 4 * 4 + dz % 4

        @pl.loop(0, 2)
        def _(i):
            at = pl.ds(pl.multiple_of(i * 256, 256), 256)
            acc[at, :] += jnp.dot(tok[source, at, :], w[slot], preferred_element_type=F32)

    for dz in (0, 3, 1, 2):
        project(0, dz)
    for dz in (0, 3, 1):
        project(1, dz)
        project(3, dz)
    h2 = x_forward(x2, 2)
    project(1, 2)
    project(3, 2)
    for pair, dz in ((h0, 0), (h3, 3), (h1, 1), (h2, 2)):
        pair[0].wait_recv()
        pair[1].wait_recv()
        project(2, dz)

    locals_[5].wait()
    locals_[6].wait()
    pair_own = acc[:, SL:WC]
    turned = pair_own * cos[...] + pltpu.roll(pair_own, HD // 2, 1) * sin[...]
    kv[c] = jnp.where(c == 0, turned, pair_own).astype(BF16)
    kv_copy = send(kv.at[c], kv.at[c], CORE)
    for n in range(4):
        one = acc[:, n * HD:(n + 1) * HD]
        q[n] = (one * cos[...] + pltpu.roll(one, HD // 2, 1) * sin[...]).astype(BF16)
    kv_copy.wait_recv()

    def position(p):
        return (p // 32) % 8 * 64 + p // 256 * 32 + p % 32

    key_at = position(lax.broadcasted_iota(jnp.int32, (1, SEQ), 1))
    scale = 1.0 / HD**0.5

    def heads(part):
        @pl.loop(0, 4)
        def _(i):
            n = i // 2
            at = pl.ds(pl.multiple_of(i % 2 * 256, 256), 256)
            query_at = position(lax.broadcasted_iota(jnp.int32, (256, 1), 0) + i % 2 * 256)
            scores = lax.dot_general(
                q[part * 2 + n, at, :], kv[0], (((1,), (1,)), ((), ())), preferred_element_type=F32) * scale
            scores = jnp.where(query_at >= key_at, scores, -1e30)
            weights = jnp.exp(scores - jnp.max(scores, axis=-1, keepdims=True))
            probs = (weights / jnp.sum(weights, axis=-1, keepdims=True)).astype(BF16)
            mixed = jnp.dot(probs, kv[1], preferred_element_type=F32).astype(BF16)
            ctx[0, part, at, pl.ds(pl.multiple_of(n * HD, HD), HD)] = mixed

    c_pairs = []
    for part in range(2):
        heads(part)
        c_pairs.append((send(ctx.at[0, part], ctx.at[3, part], x_by(1)),
                        send(ctx.at[0, part], ctx.at[1, part], x_by(-1))))
    wf0.wait_recv()
    wf1.wait_recv()

    own_rows = pl.ds(pl.multiple_of(c * 256, 256), 256)
    other_rows = pl.ds(pl.multiple_of((1 - c) * 256, 256), 256)

    def product(dx, at, m):
        return (jnp.dot(ctx[dx, 0, at, :], wo[m, pl.ds(0, 256), :], preferred_element_type=F32)
                + jnp.dot(ctx[dx, 1, at, :], wo[m, pl.ds(256, 256), :], preferred_element_type=F32)).astype(BF16)

    def partial(dx):
        @pl.loop(0, 4)
        def _(m):
            give[dx, m] = product(dx, other_rows, m)
        swap = send(give.at[dx], got.at[dx], CORE)

        @pl.loop(0, 4)
        def _(m):
            ss[dx, m] = product(dx, own_rows, m)
        swap.wait_recv()

        @pl.loop(0, 4)
        def _(m):
            ss[dx, m] = (ss[dx, m].astype(F32) + got[dx, m].astype(F32)).astype(BF16)
        sent = []
        for k, rel in enumerate(PLANE):
            block = pl.ds(pl.multiple_of(((y + rel[1]) % 4 * 2 + (zl + rel[3]) % 2) * 32, 32), 32)
            sent.append(send(ss.at[dx, :, block, :], red.at[dx, k], rel))
        return sent

    r0 = partial(0)
    forwards = []
    for part in range(2):
        c_pairs[part][0].wait_recv()
        a = send(ctx.at[3, part, pl.ds(0, 256), :], ctx.at[2, part, pl.ds(0, 256), :], x_by(1))
        c_pairs[part][1].wait_recv()
        b = send(ctx.at[1, part, pl.ds(256, 256), :], ctx.at[2, part, pl.ds(256, 256), :], x_by(-1))
        forwards += [a, b]
    r1 = partial(1)
    r3 = partial(3)
    for copy in forwards:
        copy.wait_recv()
    r2 = partial(2)

    own_block = pl.ds(pl.multiple_of(group * 32, 32), 32)
    back = []
    for dx, sent in ((0, r0), (1, r1), (3, r3), (2, r2)):
        for copy in sent:
            copy.wait_recv()

        @pl.loop(0, 4)
        def _(m):
            total = ss[dx, m, own_block, :].astype(F32)
            for k in range(len(PLANE)):
                total += red[dx, k, m].astype(F32)
            if dx == 0:
                parts[m] = total.astype(BF16)
            else:
                fin[dx, m] = total.astype(BF16)
        if dx != 0:
            back.append(send(fin.at[dx], parts.at[pl.ds((4 - dx) % 4 * 4, 4)], x_by(dx)))
    for copy in back:
        copy.wait_recv()

    for s in range(16):
        out[:, s * SL:(s + 1) * SL] = parts[slots[s]]
    for copy in copies:
        copy.wait_send()


N_COPIES = 20 + 15 + 4 + 1 + 8 + 4 * 8 + 3


def tables():
    p = np.arange(SEQ)
    where_at = ((p // 32) % 8 * 64 + p // 256 * 32 + p % 32).astype(np.float32)
    freqs = np.float32(ROPE_THETA) ** (-(np.arange(HD // 2, dtype=np.float32) * np.float32(2.0)) / np.float32(HD))
    angles = where_at[:, None] * freqs[None, :]
    cosine, sine = np.cos(angles), np.sin(angles)
    return (np.concatenate([cosine, cosine], 1).astype(np.float32),
            np.concatenate([-sine, sine], 1).astype(np.float32))


def per_device(hidden, norm_gain, q_weight, kv_weight, out_weight, held_slice):
    cosine, sine = tables()
    vm = pltpu.VMEM
    rep = lax.axis_index("rep")
    numbers = jnp.arange(16, dtype=jnp.int32)
    place = (numbers // 4 + 4 - rep // 4) % 4 * 4 + (numbers % 4 + 4 - rep % 4) % 4
    slots = jnp.sum(jnp.where(held_slice[None, :] == numbers[:, None], place[None, :], 0), axis=1)
    return pl.pallas_call(
        kernel,
        out_shape=jax.ShapeDtypeStruct((32, D), BF16),
        in_specs=[pl.BlockSpec(memory_space=pltpu.SMEM)] * 2 + [pl.BlockSpec(memory_space=pl.ANY)] * 7,
        out_specs=pl.BlockSpec(memory_space=pltpu.VMEM),
        scratch_shapes=[
            vm((32, D), BF16), vm((1, D), BF16), vm((SEQ, HD), F32), vm((SEQ, HD), F32),
            vm((16, SEQ, SL), BF16), vm((16, SL, WC), BF16), vm((4, SL, SL), BF16), vm((SEQ, WC), F32),
            vm((2, SEQ, HD), BF16), vm((4, SEQ, HD), BF16), vm((4, 2, SEQ, 256), BF16),
            vm((4, 4, 256, SL), BF16), vm((4, 4, 256, SL), BF16), vm((4, 4, 256, SL), BF16),
            vm((4, 7, 4, 32, SL), BF16), vm((4, 4, 32, SL), BF16), vm((16, 32, SL), BF16),
            pltpu.SemaphoreType.DMA((7,)), pltpu.SemaphoreType.DMA((N_COPIES,)), pltpu.SemaphoreType.DMA((N_COPIES,)),
        ],
        compiler_params=pltpu.CompilerParams(
            collective_id=0, has_side_effects=True, vmem_limit_bytes=62 * 1024 * 1024),
        name="block",
    )(held_slice, slots, hidden, norm_gain.reshape(1, D), q_weight, kv_weight, out_weight,
      jnp.asarray(cosine), jnp.asarray(sine))


def solution(mesh):
    return jax.shard_map(
        per_device,
        mesh=mesh,
        in_specs=(P(("rep", "tp"), None), P(), P("rep", "tp"), P("rep", None), P("tp", "rep"), P()),
        out_specs=P(("rep", "tp"), None),
        check_vma=False,
    )
```

```python
import jax
import jax.numpy as jnp
import numpy as np
from jax import lax
from jax.experimental import pallas as pl
from jax.experimental.pallas import tpu as pltpu
from jax.sharding import PartitionSpec as P

HD = 128
HQ = 64
KVH = 8
D = 8192
SEQ = 512
SL = 512
WC = 640
ROPE_THETA = 500000.0
MESH = pl.DeviceIdType.MESH
F32, BF16 = jnp.float32, jnp.bfloat16

CORE = (0, 0, 0, 0, 1)
ZL = (0, 0, 0, 1, 0)
PLANE = [(0, dy, 0, dz, 0) for dy in (1, 3, 2, 0) for dz in (0, 1) if (dy, dz) != (0, 0)]


def x_by(d):
    return (d % 4, 0, 0, 0, 0)


def z_by(d):
    return (0, 0, d % 4, 0, 0)


def y_by(d):
    return (0, d % 4, 0, 0, 0)


PEERS = [x_by(1), x_by(2), x_by(3), z_by(1), z_by(3), CORE] + PLANE


def kernel(held, hidden, gain, q_weight, kv_weight, out_weight, cos_hbm, sin_hbm, out,
           hid, gn, cos, sin, tok, w, wo, acc, kv, q, ctx, give, got, ss, red, fin, parts, lsem, ssem, rsem):
    rep, tp = lax.axis_index("rep"), lax.axis_index("tp")
    x, zh = rep // 4, rep % 4
    y, zl, c = tp // 4, (tp // 2) % 2, tp % 2

    def target(rel):
        dx, dy, dz, dl, dc = rel
        return (
            (x + dx) % 4 * 4 + (zh + dz) % 4,
            (y + dy) % 4 * 4 + (zl + dl) % 2 * 2 + (c + dc) % 2,
        )

    copies = []

    def send(src, dst, rel):
        k = len(copies)
        copy = pltpu.make_async_remote_copy(
            src_ref=src, dst_ref=dst, send_sem=ssem.at[k], recv_sem=rsem.at[k],
            device_id=target(rel), device_id_type=MESH)
        copy.start()
        copies.append(copy)
        return copy

    group = y * 2 + zl
    locals_ = [
        pltpu.make_async_copy(q_weight, w.at[0, :, pl.ds(0, SL)], lsem.at[0]),
        pltpu.make_async_copy(
            kv_weight.at[:, pl.ds(pl.multiple_of(c * KVH * HD + group * HD, HD), HD)],
            w.at[0, :, pl.ds(SL, HD)], lsem.at[1]),
        pltpu.make_async_copy(hidden, hid, lsem.at[2]),
        pltpu.make_async_copy(gain, gn, lsem.at[3]),
        pltpu.make_async_copy(out_weight, wo.at[0], lsem.at[4]),
        pltpu.make_async_copy(cos_hbm, cos, lsem.at[5]),
        pltpu.make_async_copy(sin_hbm, sin, lsem.at[6]),
    ]
    for copy in locals_:
        copy.start()

    barrier = pltpu.get_barrier_semaphore()
    for rel in PEERS:
        pl.semaphore_signal(barrier, inc=1, device_id=target(rel), device_id_type=MESH)
    pl.semaphore_wait(barrier, len(PEERS))

    def half(dx, dz, part):
        return w.at[dx % 4 * 4 + dz % 4, pl.ds(part * (SL // 2), SL // 2), :]

    def x_send(dz, part, d):
        return send(half(0, dz, part), half(-d, dz, part), x_by(d))

    def x_forward(copy, dz, part):
        copy.wait_recv()
        d = 1 - 2 * part
        return send(half(-d, dz, part), half(-2 * d, dz, part), x_by(d))

    locals_[0].wait()
    locals_[1].wait()
    z_first = send(half(0, 0, 0), half(0, -1, 0), z_by(1)), send(half(0, 0, 1), half(0, 1, 1), z_by(-1))
    xs = {}
    for part in range(2):
        xs[0, part, 1] = x_send(0, part, 1)
        xs[0, 1 - part, -1] = x_send(0, 1 - part, -1)

    def rows(dy, dl, dc=0):
        return pl.ds(pl.multiple_of((y + dy) % 4 * 128 + (c + dc) % 2 * 64 + (zl + dl) % 2 * 32, 32), 32)

    locals_[2].wait()
    locals_[3].wait()
    states = hid[...].astype(F32)
    factor = lax.rsqrt(jnp.mean(states * states, axis=-1, keepdims=True) + 1e-05)
    for n in range(D // HD):
        one = hid[:, n * HD:(n + 1) * HD].astype(F32) * factor * gn[n:n + 1, :].astype(F32)
        tok[n // 4, rows(0, 0), n % 4 * HD:(n % 4 + 1) * HD] = one.astype(BF16)

    def tok_at(dy, dl):
        return tok.at[:, rows(dy, dl), :]

    t_z = send(tok_at(0, 0), tok_at(0, 0), ZL)
    t_y0 = [send(tok_at(0, 0), tok_at(0, 0), y_by(d)) for d in (1, 3, 2)]
    t_core = [send(tok_at(0, 0), tok_at(0, 0), CORE)]
    z_second = send(half(0, 0, 1), half(0, -1, 1), z_by(1)), send(half(0, 0, 0), half(0, 1, 0), z_by(-1))

    ends = [(0, x_forward(xs[0, 0, 1], 0, 0), x_forward(xs[0, 1, -1], 0, 1))]
    z_first[0].wait_recv()
    zf0 = send(half(0, -1, 0), half(0, -2, 0), z_by(1))
    for d in (1, -1):
        xs[-1, 0, d] = x_send(-1, 0, d)
    z_first[1].wait_recv()
    zf1 = send(half(0, 1, 1), half(0, 2, 1), z_by(-1))
    for d in (-1, 1):
        xs[1, 1, d] = x_send(1, 1, d)
    locals_[4].wait()
    wo_pair = send(wo.at[0], wo.at[3], z_by(1)), send(wo.at[0], wo.at[1], z_by(-1))
    t_z.wait_recv()
    t_y1 = [send(tok_at(0, 1), tok_at(0, 1), y_by(d)) for d in (1, 3, 2)]
    t_core.append(send(tok_at(0, 1), tok_at(0, 1), CORE))
    for d, copy in zip((1, 3, 2), t_y0):
        copy.wait_recv()
        t_core.append(send(tok_at(-d, 0), tok_at(-d, 0), CORE))
    f30 = x_forward(xs[-1, 0, 1], -1, 0)
    f11 = x_forward(xs[1, 1, -1], 1, 1)
    z_second[0].wait_recv()
    for d in (-1, 1):
        xs[-1, 1, d] = x_send(-1, 1, d)
    z_second[1].wait_recv()
    for d in (1, -1):
        xs[1, 0, d] = x_send(1, 0, d)
    zf0.wait_recv()
    for d in (1, -1):
        xs[2, 0, d] = x_send(2, 0, d)
    zf1.wait_recv()
    for d in (-1, 1):
        xs[2, 1, d] = x_send(2, 1, d)
    ends.append((-1, f30, x_forward(xs[-1, 1, -1], -1, 1)))
    ends.append((1, x_forward(xs[1, 0, 1], 1, 0), f11))
    for d, copy in zip((1, 3, 2), t_y1):
        copy.wait_recv()
        t_core.append(send(tok_at(-d, 1), tok_at(-d, 1), CORE))
    for copy in t_core:
        copy.wait_recv()

    acc[...] = jnp.zeros_like(acc)

    def project(dx, dz):
        source = held[(x + dx) % 4 * 4 + (zh + dz) % 4]
        slot = dx % 4 * 4 + dz % 4

        @pl.loop(0, 2)
        def _(i):
            at = pl.ds(pl.multiple_of(i * 256, 256), 256)
            acc[at, :] += jnp.dot(tok[source, at, :], w[slot], preferred_element_type=F32)

    for dz in (0, -1, 1, 2):
        project(0, dz)
    for dz in (0, -1, 1):
        xs[dz, 1, 1].wait_recv()
        project(-1, dz)
        xs[dz, 0, -1].wait_recv()
        project(1, dz)
    ends.append((2, x_forward(xs[2, 0, 1], 2, 0), x_forward(xs[2, 1, -1], 2, 1)))
    wo_pair[0].wait_recv()
    wf0 = send(wo.at[3, pl.ds(0, 256), :], wo.at[2, pl.ds(0, 256), :], z_by(1))
    wo_pair[1].wait_recv()
    wf1 = send(wo.at[1, pl.ds(256, 256), :], wo.at[2, pl.ds(256, 256), :], z_by(-1))
    xs[2, 1, 1].wait_recv()
    project(-1, 2)
    xs[2, 0, -1].wait_recv()
    project(1, 2)
    for dz, a, b in ends:
        a.wait_recv()
        b.wait_recv()
        project(2, dz)

    locals_[5].wait()
    locals_[6].wait()
    pair_own = acc[:, SL:WC]
    turned = pair_own * cos[...] + pltpu.roll(pair_own, HD // 2, 1) * sin[...]
    kv[c] = jnp.where(c == 0, turned, pair_own).astype(BF16)
    kv_copy = send(kv.at[c], kv.at[c], CORE)
    for n in range(4):
        one = acc[:, n * HD:(n + 1) * HD]
        q[n] = (one * cos[...] + pltpu.roll(one, HD // 2, 1) * sin[...]).astype(BF16)
    kv_copy.wait_recv()

    def position(p):
        return p // 32 % 2 * 64 + p // 64 * 32 + p % 32

    earlier = (position(lax.broadcasted_iota(jnp.int32, (HD, 1), 0))
               >= position(lax.broadcasted_iota(jnp.int32, (1, HD), 1)))
    scale = HD**-0.5 / np.log(2.0)

    def heads(part):
        for n in range(2):
            for b in range(4):
                end = (b + 1) * 128
                scores = lax.dot_general(
                    q[part * 2 + n, b * 128:end, :], kv[0, :end, :], (((1,), (1,)), ((), ())),
                    preferred_element_type=F32)
                near = jnp.where(earlier, scores[:, end - 128:], -1e30)
                scores = jnp.concatenate([scores[:, :end - 128], near], axis=1) if b else near
                weights = jnp.exp2((scores - jnp.max(scores, axis=-1, keepdims=True)) * scale)
                probs = (weights * (1.0 / jnp.sum(weights, axis=-1, keepdims=True))).astype(BF16)
                mixed = jnp.dot(probs, kv[1, :end, :], preferred_element_type=F32).astype(BF16)
                ctx[0, part, b, :, :, n * HD:(n + 1) * HD] = mixed.reshape(2, 64, HD)

    c_pairs = []
    for part in range(2):
        heads(part)
        c_pairs.append((send(ctx.at[0, part], ctx.at[3, part], x_by(1)),
                        send(ctx.at[0, part], ctx.at[1, part], x_by(-1))))
    wf0.wait_recv()
    wf1.wait_recv()

    def product(dx, core, m):
        first, second = (ctx[dx, part, :, core].reshape(256, 256) for part in range(2))
        return (jnp.dot(first, wo[m, pl.ds(0, 256), :], preferred_element_type=F32)
                + jnp.dot(second, wo[m, pl.ds(256, 256), :], preferred_element_type=F32)).astype(BF16)

    def partial(dx):
        @pl.loop(0, 4)
        def _(m):
            give[dx, m] = product(dx, 1 - c, m)
        swap = send(give.at[dx], got.at[dx], CORE)

        @pl.loop(0, 4)
        def _(m):
            ss[dx, m] = product(dx, c, m)
        swap.wait_recv()

        @pl.loop(0, 4)
        def _(m):
            ss[dx, m] = (ss[dx, m].astype(F32) + got[dx, m].astype(F32)).astype(BF16)
        sent = []
        for k, rel in enumerate(PLANE):
            block = pl.ds(pl.multiple_of(((y + rel[1]) % 4 * 2 + (zl + rel[3]) % 2) * 32, 32), 32)
            sent.append(send(ss.at[dx, :, block, :], red.at[dx, k], rel))
        return sent

    r0 = partial(0)
    forwards = []
    for part in range(2):
        c_pairs[part][0].wait_recv()
        a = send(ctx.at[3, part, pl.ds(0, 2)], ctx.at[2, part, pl.ds(0, 2)], x_by(1))
        c_pairs[part][1].wait_recv()
        b = send(ctx.at[1, part, pl.ds(2, 2)], ctx.at[2, part, pl.ds(2, 2)], x_by(-1))
        forwards += [a, b]
    r1 = partial(1)
    r3 = partial(3)
    for copy in forwards:
        copy.wait_recv()
    r2 = partial(2)

    own_block = pl.ds(pl.multiple_of(group * 32, 32), 32)
    back = []
    for dx, sent in ((0, r0), (1, r1), (3, r3), (2, r2)):
        for copy in sent:
            copy.wait_recv()

        @pl.loop(0, 4)
        def _(m):
            total = ss[dx, m, own_block, :].astype(F32)
            for k in range(len(PLANE)):
                total += red[dx, k, m].astype(F32)
            if dx == 0:
                parts[m] = total.astype(BF16)
            else:
                fin[dx, m] = total.astype(BF16)
        if dx != 0:
            back.append(send(fin.at[dx], parts.at[pl.ds((4 - dx) % 4 * 4, 4)], x_by(dx)))
    for copy in back:
        copy.wait_recv()

    out[...] = parts[...]
    for copy in copies:
        copy.wait_send()


def place(held, parts, out):
    rep = lax.axis_index("rep")
    for r in range(16):
        slot = (r // 4 + 4 - rep // 4) % 4 * 4 + (r % 4 + 4 - rep % 4) % 4
        out[:, pl.ds(pl.multiple_of(held[r] * SL, SL), SL)] = parts[slot]


N_COPIES = 30 + 15 + 4 + 1 + 8 + 4 * 8 + 3


def tables():
    p = np.arange(SEQ)
    where_at = (p // 128 * 128 + p // 32 % 2 * 64 + p // 64 % 2 * 32 + p % 32).astype(np.float32)
    freqs = np.float32(ROPE_THETA) ** (-(np.arange(HD // 2, dtype=np.float32) * np.float32(2.0)) / np.float32(HD))
    angles = where_at[:, None] * freqs[None, :]
    cosine, sine = np.cos(angles), np.sin(angles)
    return (np.concatenate([cosine, cosine], 1).astype(np.float32),
            np.concatenate([-sine, sine], 1).astype(np.float32))


def per_device(hidden, norm_gain, q_weight, kv_weight, out_weight, held_slice):
    cosine, sine = tables()
    vm = pltpu.VMEM
    parts = pl.pallas_call(
        kernel,
        out_shape=jax.ShapeDtypeStruct((16, 32, SL), BF16),
        in_specs=[pl.BlockSpec(memory_space=pltpu.SMEM)] + [pl.BlockSpec(memory_space=pl.ANY)] * 7,
        out_specs=pl.BlockSpec(memory_space=pltpu.VMEM),
        scratch_shapes=[
            vm((32, D), BF16), vm((D // HD, HD), BF16), vm((SEQ, HD), F32), vm((SEQ, HD), F32),
            vm((16, SEQ, SL), BF16), vm((16, SL, WC), BF16), vm((4, SL, SL), BF16), vm((SEQ, WC), F32),
            vm((2, SEQ, HD), BF16), vm((4, SEQ, HD), BF16), vm((4, 2, 4, 2, 64, 256), BF16),
            vm((4, 4, 256, SL), BF16), vm((4, 4, 256, SL), BF16), vm((4, 4, 256, SL), BF16),
            vm((4, 7, 4, 32, SL), BF16), vm((4, 4, 32, SL), BF16), vm((16, 32, SL), BF16),
            pltpu.SemaphoreType.DMA((7,)), pltpu.SemaphoreType.DMA((N_COPIES,)), pltpu.SemaphoreType.DMA((N_COPIES,)),
        ],
        compiler_params=pltpu.CompilerParams(
            collective_id=0, has_side_effects=True, vmem_limit_bytes=62 * 1024 * 1024),
        name="block",
    )(held_slice, hidden, norm_gain.reshape(D // HD, HD), q_weight, kv_weight, out_weight,
      jnp.asarray(cosine), jnp.asarray(sine))
    return pl.pallas_call(
        place,
        out_shape=jax.ShapeDtypeStruct((32, D), BF16),
        in_specs=[pl.BlockSpec(memory_space=pltpu.SMEM), pl.BlockSpec(memory_space=pltpu.VMEM)],
        out_specs=pl.BlockSpec(memory_space=pltpu.VMEM),
        name="place",
    )(held_slice, parts)


def solution(mesh):
    return jax.shard_map(
        per_device,
        mesh=mesh,
        in_specs=(P(("rep", "tp"), None), P(), P("rep", "tp"), P("rep", None), P("tp", "rep"), P()),
        out_specs=P(("rep", "tp"), None),
        check_vma=False,
    )
```

```python
import jax
import jax.numpy as jnp
import numpy as np
from jax import lax
from jax.experimental import pallas as pl
from jax.experimental.pallas import tpu as pltpu
from jax.sharding import PartitionSpec as P

HD = 128
HQ = 64
KVH = 8
D = 8192
SEQ = 512
SL = 512
WC = 640
ROPE_THETA = 500000.0
MESH = pl.DeviceIdType.MESH
F32, BF16 = jnp.float32, jnp.bfloat16

CORE = (0, 0, 0, 0, 1)
ZL = (0, 0, 0, 1, 0)
PLANE = [(0, 1, 0, 0, 0), (0, 3, 0, 0, 0), (0, 1, 0, 1, 0), (0, 3, 0, 1, 0), ZL]


def x_by(d):
    return (d % 4, 0, 0, 0, 0)


def z_by(d):
    return (0, 0, d % 4, 0, 0)


def y_by(d):
    return (0, d % 4, 0, 0, 0)


PEERS = [x_by(1), x_by(2), x_by(3), z_by(1), z_by(3), y_by(2), CORE] + PLANE


def kernel(held, hidden, gain, q_weight, kv_weight, out_weight, cos_hbm, sin_hbm, out,
           hid, gn, cos, sin, tok, w, wo, acc, kv, q, ctx, give, got, ss, via, red, fin, parts, lsem, ssem, rsem):
    rep, tp = lax.axis_index("rep"), lax.axis_index("tp")
    x, zh = rep // 4, rep % 4
    y, zl, c = tp // 4, (tp // 2) % 2, tp % 2

    def target(rel):
        dx, dy, dz, dl, dc = rel
        return (
            (x + dx) % 4 * 4 + (zh + dz) % 4,
            (y + dy) % 4 * 4 + (zl + dl) % 2 * 2 + (c + dc) % 2,
        )

    copies = []

    def send(src, dst, rel):
        k = len(copies)
        copy = pltpu.make_async_remote_copy(
            src_ref=src, dst_ref=dst, send_sem=ssem.at[k], recv_sem=rsem.at[k],
            device_id=target(rel), device_id_type=MESH)
        copy.start()
        copies.append(copy)
        return copy

    group = y * 2 + zl
    locals_ = [
        pltpu.make_async_copy(q_weight, w.at[0, :, pl.ds(0, SL)], lsem.at[0]),
        pltpu.make_async_copy(
            kv_weight.at[:, pl.ds(pl.multiple_of(c * KVH * HD + group * HD, HD), HD)],
            w.at[0, :, pl.ds(SL, HD)], lsem.at[1]),
        pltpu.make_async_copy(hidden, hid, lsem.at[2]),
        pltpu.make_async_copy(gain, gn, lsem.at[3]),
        pltpu.make_async_copy(out_weight, wo.at[0], lsem.at[4]),
        pltpu.make_async_copy(cos_hbm, cos, lsem.at[5]),
        pltpu.make_async_copy(sin_hbm, sin, lsem.at[6]),
    ]
    for copy in locals_:
        copy.start()

    barrier = pltpu.get_barrier_semaphore()
    for rel in PEERS:
        pl.semaphore_signal(barrier, inc=1, device_id=target(rel), device_id_type=MESH)
    pl.semaphore_wait(barrier, len(PEERS))

    def half(dx, dz, part):
        return w.at[dx % 4 * 4 + dz % 4, pl.ds(part * (SL // 2), SL // 2), :]

    def x_send(dz, part, d):
        return send(half(0, dz, part), half(-d, dz, part), x_by(d))

    def x_forward(copy, dz, part):
        copy.wait_recv()
        d = 1 - 2 * part
        return send(half(-d, dz, part), half(-2 * d, dz, part), x_by(d))

    locals_[0].wait()
    locals_[1].wait()
    z_first = send(half(0, 0, 0), half(0, -1, 0), z_by(1)), send(half(0, 0, 1), half(0, 1, 1), z_by(-1))
    xs = {}
    for part in range(2):
        xs[0, part, 1] = x_send(0, part, 1)
        xs[0, 1 - part, -1] = x_send(0, 1 - part, -1)

    def rows(dy, dl, dc=0):
        return pl.ds(pl.multiple_of((y + dy) % 4 * 128 + (c + dc) % 2 * 64 + (zl + dl) % 2 * 32, 32), 32)

    locals_[2].wait()
    locals_[3].wait()
    states = hid[...].astype(F32)
    factor = lax.rsqrt(jnp.mean(states * states, axis=-1, keepdims=True) + 1e-05)
    for n in range(D // HD):
        one = hid[:, n * HD:(n + 1) * HD].astype(F32) * factor * gn[n:n + 1, :].astype(F32)
        tok[n // 4, rows(0, 0), n % 4 * HD:(n % 4 + 1) * HD] = one.astype(BF16)

    def tok_at(dy, dl):
        return tok.at[:, rows(dy, dl), :]

    t_z = send(tok_at(0, 0), tok_at(0, 0), ZL)
    t_y0 = [send(tok_at(0, 0), tok_at(0, 0), y_by(d)) for d in (1, 3, 2)]
    t_core = [send(tok_at(0, 0), tok_at(0, 0), CORE)]
    z_second = send(half(0, 0, 1), half(0, -1, 1), z_by(1)), send(half(0, 0, 0), half(0, 1, 0), z_by(-1))

    ends = [(0, x_forward(xs[0, 0, 1], 0, 0), x_forward(xs[0, 1, -1], 0, 1))]
    z_first[0].wait_recv()
    zf0 = send(half(0, -1, 0), half(0, -2, 0), z_by(1))
    for d in (1, -1):
        xs[-1, 0, d] = x_send(-1, 0, d)
    z_first[1].wait_recv()
    zf1 = send(half(0, 1, 1), half(0, 2, 1), z_by(-1))
    for d in (-1, 1):
        xs[1, 1, d] = x_send(1, 1, d)
    t_z.wait_recv()
    t_y1 = [send(tok_at(0, 1), tok_at(0, 1), y_by(d)) for d in (1, 3, 2)]
    t_core.append(send(tok_at(0, 1), tok_at(0, 1), CORE))
    for d, copy in zip((1, 3, 2), t_y0):
        copy.wait_recv()
        t_core.append(send(tok_at(-d, 0), tok_at(-d, 0), CORE))
    f30 = x_forward(xs[-1, 0, 1], -1, 0)
    f11 = x_forward(xs[1, 1, -1], 1, 1)
    z_second[0].wait_recv()
    for d in (-1, 1):
        xs[-1, 1, d] = x_send(-1, 1, d)
    z_second[1].wait_recv()
    for d in (1, -1):
        xs[1, 0, d] = x_send(1, 0, d)
    zf0.wait_recv()
    for d in (1, -1):
        xs[2, 0, d] = x_send(2, 0, d)
    zf1.wait_recv()
    for d in (-1, 1):
        xs[2, 1, d] = x_send(2, 1, d)
    locals_[4].wait()
    wo_pair = send(wo.at[0], wo.at[3], z_by(1)), send(wo.at[0], wo.at[1], z_by(-1))
    ends.append((-1, f30, x_forward(xs[-1, 1, -1], -1, 1)))
    ends.append((1, x_forward(xs[1, 0, 1], 1, 0), f11))
    for d, copy in zip((1, 3, 2), t_y1):
        copy.wait_recv()
        t_core.append(send(tok_at(-d, 1), tok_at(-d, 1), CORE))
    for copy in t_core:
        copy.wait_recv()

    acc[...] = jnp.zeros_like(acc)

    def project(dx, dz):
        source = held[(x + dx) % 4 * 4 + (zh + dz) % 4]
        slot = dx % 4 * 4 + dz % 4

        @pl.loop(0, 2)
        def _(i):
            at = pl.ds(pl.multiple_of(i * 256, 256), 256)
            acc[at, :] += jnp.dot(tok[source, at, :], w[slot], preferred_element_type=F32)

    for dz in (0, -1, 1, 2):
        project(0, dz)
    for dz in (0, -1, 1):
        xs[dz, 1, 1].wait_recv()
        project(-1, dz)
        xs[dz, 0, -1].wait_recv()
        project(1, dz)
    ends.append((2, x_forward(xs[2, 0, 1], 2, 0), x_forward(xs[2, 1, -1], 2, 1)))
    wo_pair[0].wait_recv()
    wf0 = send(wo.at[3, pl.ds(0, 256), :], wo.at[2, pl.ds(0, 256), :], z_by(1))
    wo_pair[1].wait_recv()
    wf1 = send(wo.at[1, pl.ds(256, 256), :], wo.at[2, pl.ds(256, 256), :], z_by(-1))
    xs[2, 1, 1].wait_recv()
    project(-1, 2)
    xs[2, 0, -1].wait_recv()
    project(1, 2)
    for dz, a, b in ends:
        a.wait_recv()
        b.wait_recv()
        project(2, dz)

    locals_[5].wait()
    locals_[6].wait()
    pair_own = acc[:, SL:WC]
    turned = pair_own * cos[...] + pltpu.roll(pair_own, HD // 2, 1) * sin[...]
    kv[c] = jnp.where(c == 0, turned, pair_own).astype(BF16)
    kv_copy = send(kv.at[c], kv.at[c], CORE)
    for n in range(4):
        one = acc[:, n * HD:(n + 1) * HD]
        q[n] = (one * cos[...] + pltpu.roll(one, HD // 2, 1) * sin[...]).astype(BF16)
    kv_copy.wait_recv()

    def position(p):
        return p // 32 % 2 * 64 + p // 64 * 32 + p % 32

    earlier = (position(lax.broadcasted_iota(jnp.int32, (HD, 1), 0))
               >= position(lax.broadcasted_iota(jnp.int32, (1, HD), 1)))
    scale = HD**-0.5 / np.log(2.0)

    def heads(part):
        for n in range(2):
            for b in range(4):
                end = (b + 1) * 128
                scores = lax.dot_general(
                    q[part * 2 + n, b * 128:end, :], kv[0, :end, :], (((1,), (1,)), ((), ())),
                    preferred_element_type=F32)
                near = jnp.where(earlier, scores[:, end - 128:], -1e30)
                scores = jnp.concatenate([scores[:, :end - 128], near], axis=1) if b else near
                weights = jnp.exp2((scores - jnp.max(scores, axis=-1, keepdims=True)) * scale)
                probs = (weights * (1.0 / jnp.sum(weights, axis=-1, keepdims=True))).astype(BF16)
                mixed = jnp.dot(probs, kv[1, :end, :], preferred_element_type=F32).astype(BF16)
                ctx[0, part, b, :, :, n * HD:(n + 1) * HD] = mixed.reshape(2, 64, HD)

    c_pairs = []
    for part in range(2):
        heads(part)
        c_pairs.append((send(ctx.at[0, part], ctx.at[3, part], x_by(1)),
                        send(ctx.at[0, part], ctx.at[1, part], x_by(-1))))
    wf0.wait_recv()
    wf1.wait_recv()

    def product(dx, core, m):
        first, second = (ctx[dx, part, :, core].reshape(256, 256) for part in range(2))
        return (jnp.dot(first, wo[m, pl.ds(0, 256), :], preferred_element_type=F32)
                + jnp.dot(second, wo[m, pl.ds(256, 256), :], preferred_element_type=F32)).astype(BF16)

    def partial(dx):
        @pl.loop(0, 4)
        def _(m):
            give[dx, m] = product(dx, 1 - c, m)
        swap = send(give.at[dx], got.at[dx], CORE)

        @pl.loop(0, 4)
        def _(m):
            ss[dx, m] = product(dx, c, m)
        swap.wait_recv()

        @pl.loop(0, 4)
        def _(m):
            ss[dx, m] = (ss[dx, m].astype(F32) + got[dx, m].astype(F32)).astype(BF16)
        return [
            send(ss.at[dx, pl.ds(0, 2), y_rows(2), :], via.at[dx, 0], y_by(1)),
            send(ss.at[dx, pl.ds(2, 2), y_rows(2), :], via.at[dx, 1], y_by(-1)),
            to_owner(dx, 4),
        ]

    def y_rows(d):
        return pl.ds(pl.multiple_of((y + d) % 4 * 64, 64), 64)

    def to_owner(dx, k):
        rel = PLANE[k]
        block = pl.ds(pl.multiple_of((y + rel[1]) % 4 * 64 + (zl + rel[3]) % 2 * 32, 32), 32)
        return send(ss.at[dx, :, block, :], red.at[dx, k], rel)

    def pass_on(dx, first):
        sent = [first[2]]
        for part, d in ((0, 1), (1, 3)):
            first[part].wait_recv()
            for m in range(2):
                at = (dx, part * 2 + m, y_rows(d), slice(None))
                ss[at] = (ss[at].astype(F32) + via[dx, part, m].astype(F32)).astype(BF16)
            sent += [to_owner(dx, part), to_owner(dx, part + 2)]
        return sent

    r0 = pass_on(0, partial(0))
    forwards = []
    for part in range(2):
        c_pairs[part][0].wait_recv()
        a = send(ctx.at[3, part, pl.ds(0, 2)], ctx.at[2, part, pl.ds(0, 2)], x_by(1))
        c_pairs[part][1].wait_recv()
        b = send(ctx.at[1, part, pl.ds(2, 2)], ctx.at[2, part, pl.ds(2, 2)], x_by(-1))
        forwards += [a, b]
    first1 = partial(1)
    first3 = partial(3)
    r1 = pass_on(1, first1)
    r3 = pass_on(3, first3)
    for copy in forwards:
        copy.wait_recv()
    r2 = pass_on(2, partial(2))

    own_block = pl.ds(pl.multiple_of(group * 32, 32), 32)
    back = []
    for dx, sent in ((0, r0), (1, r1), (3, r3), (2, r2)):
        for copy in sent:
            copy.wait_recv()

        @pl.loop(0, 4)
        def _(m):
            total = ss[dx, m, own_block, :].astype(F32)
            for k in range(len(PLANE)):
                total += red[dx, k, m].astype(F32)
            if dx == 0:
                parts[m] = total.astype(BF16)
            else:
                fin[dx, m] = total.astype(BF16)
        if dx != 0:
            back.append(send(fin.at[dx], parts.at[pl.ds((4 - dx) % 4 * 4, 4)], x_by(dx)))
    for copy in back:
        copy.wait_recv()

    out[...] = parts[...]
    for copy in copies:
        copy.wait_send()


def place(held, parts, out):
    rep = lax.axis_index("rep")
    for r in range(16):
        slot = (r // 4 + 4 - rep // 4) % 4 * 4 + (r % 4 + 4 - rep % 4) % 4
        out[:, pl.ds(pl.multiple_of(held[r] * SL, SL), SL)] = parts[slot]


N_COPIES = 30 + 15 + 4 + 1 + 8 + 4 * 8 + 3


def tables():
    p = np.arange(SEQ)
    where_at = (p // 128 * 128 + p // 32 % 2 * 64 + p // 64 % 2 * 32 + p % 32).astype(np.float32)
    freqs = np.float32(ROPE_THETA) ** (-(np.arange(HD // 2, dtype=np.float32) * np.float32(2.0)) / np.float32(HD))
    angles = where_at[:, None] * freqs[None, :]
    cosine, sine = np.cos(angles), np.sin(angles)
    return (np.concatenate([cosine, cosine], 1).astype(np.float32),
            np.concatenate([-sine, sine], 1).astype(np.float32))


def per_device(hidden, norm_gain, q_weight, kv_weight, out_weight, held_slice):
    cosine, sine = tables()
    vm = pltpu.VMEM
    parts = pl.pallas_call(
        kernel,
        out_shape=jax.ShapeDtypeStruct((16, 32, SL), BF16),
        in_specs=[pl.BlockSpec(memory_space=pltpu.SMEM)] + [pl.BlockSpec(memory_space=pl.ANY)] * 7,
        out_specs=pl.BlockSpec(memory_space=pltpu.VMEM),
        scratch_shapes=[
            vm((32, D), BF16), vm((D // HD, HD), BF16), vm((SEQ, HD), F32), vm((SEQ, HD), F32),
            vm((16, SEQ, SL), BF16), vm((16, SL, WC), BF16), vm((4, SL, SL), BF16), vm((SEQ, WC), F32),
            vm((2, SEQ, HD), BF16), vm((4, SEQ, HD), BF16), vm((4, 2, 4, 2, 64, 256), BF16),
            vm((4, 4, 256, SL), BF16), vm((4, 4, 256, SL), BF16), vm((4, 4, 256, SL), BF16),
            vm((4, 2, 2, 64, SL), BF16), vm((4, 5, 4, 32, SL), BF16), vm((4, 4, 32, SL), BF16), vm((16, 32, SL), BF16),
            pltpu.SemaphoreType.DMA((7,)), pltpu.SemaphoreType.DMA((N_COPIES,)), pltpu.SemaphoreType.DMA((N_COPIES,)),
        ],
        compiler_params=pltpu.CompilerParams(
            collective_id=0, has_side_effects=True, vmem_limit_bytes=62 * 1024 * 1024),
        name="block",
    )(held_slice, hidden, norm_gain.reshape(D // HD, HD), q_weight, kv_weight, out_weight,
      jnp.asarray(cosine), jnp.asarray(sine))
    return pl.pallas_call(
        place,
        out_shape=jax.ShapeDtypeStruct((32, D), BF16),
        in_specs=[pl.BlockSpec(memory_space=pltpu.SMEM), pl.BlockSpec(memory_space=pltpu.VMEM)],
        out_specs=pl.BlockSpec(memory_space=pltpu.VMEM),
        name="place",
    )(held_slice, parts)


def solution(mesh):
    return jax.shard_map(
        per_device,
        mesh=mesh,
        in_specs=(P(("rep", "tp"), None), P(), P("rep", "tp"), P("rep", None), P("tp", "rep"), P()),
        out_specs=P(("rep", "tp"), None),
        check_vma=False,
    )
```

```python
import jax
import jax.numpy as jnp
import numpy as np
from jax import lax
from jax.experimental import pallas as pl
from jax.experimental.pallas import tpu as pltpu
from jax.sharding import PartitionSpec as P

HD = 128
HQ = 64
KVH = 8
D = 8192
SEQ = 512
SL = 512
WC = 640
ROPE_THETA = 500000.0
MESH = pl.DeviceIdType.MESH
F32, BF16 = jnp.float32, jnp.bfloat16

CORE = (0, 0, 0, 0, 1)
ZL = (0, 0, 0, 1, 0)
PLANE = [(0, 1, 0, 0, 0), (0, 3, 0, 0, 0), (0, 1, 0, 1, 0), (0, 3, 0, 1, 0), ZL]


def x_by(d):
    return (d % 4, 0, 0, 0, 0)


def z_by(d):
    return (0, 0, d % 4, 0, 0)


def y_by(d):
    return (0, d % 4, 0, 0, 0)


PEERS = [x_by(1), x_by(2), x_by(3), z_by(1), z_by(3), y_by(2), CORE] + PLANE


def kernel(held, hidden, gain, q_weight, kv_weight, out_weight, cos_hbm, sin_hbm, out,
           hid, gn, cos, sin, tok, w, wo, acc, kv, q, ctx, give, got, ss, via, red, fin, parts, lsem, ssem, rsem):
    rep, tp = lax.axis_index("rep"), lax.axis_index("tp")
    x, zh = rep // 4, rep % 4
    y, zl, c = tp // 4, (tp // 2) % 2, tp % 2

    def target(rel):
        dx, dy, dz, dl, dc = rel
        return (
            (x + dx) % 4 * 4 + (zh + dz) % 4,
            (y + dy) % 4 * 4 + (zl + dl) % 2 * 2 + (c + dc) % 2,
        )

    copies = []

    def send(src, dst, rel):
        k = len(copies)
        copy = pltpu.make_async_remote_copy(
            src_ref=src, dst_ref=dst, send_sem=ssem.at[k], recv_sem=rsem.at[k],
            device_id=target(rel), device_id_type=MESH)
        copy.start()
        copies.append(copy)
        return copy

    group = y * 2 + zl
    locals_ = [
        pltpu.make_async_copy(q_weight, w.at[0, :, pl.ds(0, SL)], lsem.at[0]),
        pltpu.make_async_copy(
            kv_weight.at[:, pl.ds(pl.multiple_of(c * KVH * HD + group * HD, HD), HD)],
            w.at[0, :, pl.ds(SL, HD)], lsem.at[1]),
        pltpu.make_async_copy(hidden, hid, lsem.at[2]),
        pltpu.make_async_copy(gain, gn, lsem.at[3]),
        pltpu.make_async_copy(out_weight, wo.at[0], lsem.at[4]),
        pltpu.make_async_copy(cos_hbm, cos, lsem.at[5]),
        pltpu.make_async_copy(sin_hbm, sin, lsem.at[6]),
    ]
    for copy in locals_:
        copy.start()

    barrier = pltpu.get_barrier_semaphore()
    for rel in PEERS:
        pl.semaphore_signal(barrier, inc=1, device_id=target(rel), device_id_type=MESH)
    pl.semaphore_wait(barrier, len(PEERS))

    def half(dx, dz, part):
        return w.at[dx % 4 * 4 + dz % 4, pl.ds(part * (SL // 2), SL // 2), :]

    def x_send(dz, part, d):
        return send(half(0, dz, part), half(-d, dz, part), x_by(d))

    def x_forward(copy, dz, part):
        copy.wait_recv()
        d = 1 - 2 * part
        return send(half(-d, dz, part), half(-2 * d, dz, part), x_by(d))

    locals_[0].wait()
    locals_[1].wait()
    z_first = send(half(0, 0, 0), half(0, -1, 0), z_by(1)), send(half(0, 0, 1), half(0, 1, 1), z_by(-1))
    xs = {}
    for part in range(2):
        xs[0, part, 1] = x_send(0, part, 1)
        xs[0, 1 - part, -1] = x_send(0, 1 - part, -1)

    def rows(dy, dl, dc=0):
        return pl.ds(pl.multiple_of((y + dy) % 4 * 128 + (c + dc) % 2 * 64 + (zl + dl) % 2 * 32, 32), 32)

    locals_[2].wait()
    locals_[3].wait()
    states = hid[...].astype(F32)
    factor = lax.rsqrt(jnp.mean(states * states, axis=-1, keepdims=True) + 1e-05)
    for n in range(D // HD):
        one = hid[:, n * HD:(n + 1) * HD].astype(F32) * factor * gn[n:n + 1, :].astype(F32)
        tok[n // 4, rows(0, 0), n % 4 * HD:(n % 4 + 1) * HD] = one.astype(BF16)

    def tok_at(dy, dl):
        return tok.at[:, rows(dy, dl), :]

    t_z = send(tok_at(0, 0), tok_at(0, 0), ZL)
    t_y0 = [send(tok_at(0, 0), tok_at(0, 0), y_by(d)) for d in (1, 3, 2)]
    t_core = [send(tok_at(0, 0), tok_at(0, 0), CORE)]
    z_second = send(half(0, 0, 1), half(0, -1, 1), z_by(1)), send(half(0, 0, 0), half(0, 1, 0), z_by(-1))

    ends = [(0, x_forward(xs[0, 0, 1], 0, 0), x_forward(xs[0, 1, -1], 0, 1))]
    z_first[0].wait_recv()
    zf0 = send(half(0, -1, 0), half(0, -2, 0), z_by(1))
    for d in (1, -1):
        xs[-1, 0, d] = x_send(-1, 0, d)
    z_first[1].wait_recv()
    zf1 = send(half(0, 1, 1), half(0, 2, 1), z_by(-1))
    for d in (-1, 1):
        xs[1, 1, d] = x_send(1, 1, d)
    t_z.wait_recv()
    t_y1 = [send(tok_at(0, 1), tok_at(0, 1), y_by(d)) for d in (1, 3, 2)]
    t_core.append(send(tok_at(0, 1), tok_at(0, 1), CORE))
    for d, copy in zip((1, 3, 2), t_y0):
        copy.wait_recv()
        t_core.append(send(tok_at(-d, 0), tok_at(-d, 0), CORE))
    f30 = x_forward(xs[-1, 0, 1], -1, 0)
    f11 = x_forward(xs[1, 1, -1], 1, 1)
    z_second[0].wait_recv()
    for d in (-1, 1):
        xs[-1, 1, d] = x_send(-1, 1, d)
    z_second[1].wait_recv()
    for d in (1, -1):
        xs[1, 0, d] = x_send(1, 0, d)
    zf0.wait_recv()
    for d in (1, -1):
        xs[2, 0, d] = x_send(2, 0, d)
    zf1.wait_recv()
    for d in (-1, 1):
        xs[2, 1, d] = x_send(2, 1, d)
    locals_[4].wait()
    wo_pair = send(wo.at[0], wo.at[3], z_by(1)), send(wo.at[0], wo.at[1], z_by(-1))
    ends.append((-1, f30, x_forward(xs[-1, 1, -1], -1, 1)))
    ends.append((1, x_forward(xs[1, 0, 1], 1, 0), f11))
    for d, copy in zip((1, 3, 2), t_y1):
        copy.wait_recv()
        t_core.append(send(tok_at(-d, 1), tok_at(-d, 1), CORE))
    for copy in t_core:
        copy.wait_recv()

    acc[...] = jnp.zeros_like(acc)

    def project(dx, dz):
        source = held[(x + dx) % 4 * 4 + (zh + dz) % 4]
        slot = dx % 4 * 4 + dz % 4

        @pl.loop(0, 2)
        def _(i):
            at = pl.ds(pl.multiple_of(i * 256, 256), 256)
            acc[at, :] += jnp.dot(tok[source, at, :], w[slot], preferred_element_type=F32)

    for dz in (0, -1, 1, 2):
        project(0, dz)
    for dz in (0, -1, 1):
        xs[dz, 1, 1].wait_recv()
        project(-1, dz)
        xs[dz, 0, -1].wait_recv()
        project(1, dz)
    ends.append((2, x_forward(xs[2, 0, 1], 2, 0), x_forward(xs[2, 1, -1], 2, 1)))
    wo_pair[0].wait_recv()
    wf0 = send(wo.at[3, pl.ds(0, 256), :], wo.at[2, pl.ds(0, 256), :], z_by(1))
    wo_pair[1].wait_recv()
    wf1 = send(wo.at[1, pl.ds(256, 256), :], wo.at[2, pl.ds(256, 256), :], z_by(-1))
    xs[2, 1, 1].wait_recv()
    project(-1, 2)
    xs[2, 0, -1].wait_recv()
    project(1, 2)
    for dz, a, b in ends:
        a.wait_recv()
        b.wait_recv()
        project(2, dz)

    locals_[5].wait()
    locals_[6].wait()
    pair_own = acc[:, SL:WC]
    turned = pair_own * cos[...] + pltpu.roll(pair_own, HD // 2, 1) * sin[...]
    kv[c] = jnp.where(c == 0, turned, pair_own).astype(BF16)
    kv_copy = send(kv.at[c], kv.at[c], CORE)
    for n in range(4):
        one = acc[:, n * HD:(n + 1) * HD]
        q[n] = (one * cos[...] + pltpu.roll(one, HD // 2, 1) * sin[...]).astype(BF16)
    kv_copy.wait_recv()

    def position(p):
        return p // 32 % 2 * 64 + p // 64 * 32 + p % 32

    earlier = (position(lax.broadcasted_iota(jnp.int32, (HD, 1), 0))
               >= position(lax.broadcasted_iota(jnp.int32, (1, HD), 1)))
    scale = HD**-0.5 / np.log(2.0)

    def heads(part):
        for n in range(2):
            for b in range(4):
                end = (b + 1) * 128
                scores = lax.dot_general(
                    q[part * 2 + n, b * 128:end, :], kv[0, :end, :], (((1,), (1,)), ((), ())),
                    preferred_element_type=F32)
                near = jnp.where(earlier, scores[:, end - 128:], -1e30)
                scores = jnp.concatenate([scores[:, :end - 128], near], axis=1) if b else near
                weights = jnp.exp2((scores - jnp.max(scores, axis=-1, keepdims=True)) * scale)
                probs = (weights * (1.0 / jnp.sum(weights, axis=-1, keepdims=True))).astype(BF16)
                mixed = jnp.dot(probs, kv[1, :end, :], preferred_element_type=F32).astype(BF16)
                ctx[0, part, b, :, :, n * HD:(n + 1) * HD] = mixed.reshape(2, 64, HD)

    c_pairs = []
    for part in range(2):
        heads(part)
        c_pairs.append((send(ctx.at[0, part], ctx.at[3, part], x_by(1)),
                        send(ctx.at[0, part], ctx.at[1, part], x_by(-1))))
    wf0.wait_recv()
    wf1.wait_recv()

    def product(dx, core, m):
        first, second = (ctx[dx, part, :, core].reshape(256, 256) for part in range(2))
        return (jnp.dot(first, wo[m, pl.ds(0, 256), :], preferred_element_type=F32)
                + jnp.dot(second, wo[m, pl.ds(256, 256), :], preferred_element_type=F32)).astype(BF16)

    def y_rows(d):
        return pl.ds(pl.multiple_of((y + d) % 4 * 64, 64), 64)

    def partial(dx, lo, hi):
        @pl.loop(lo, hi)
        def _(m):
            give[dx, m] = product(dx, 1 - c, m)
        at = pl.ds(lo, hi - lo)
        swap = send(give.at[dx, at], got.at[dx, at], CORE)

        @pl.loop(lo, hi)
        def _(m):
            ss[dx, m] = product(dx, c, m)
        swap.wait_recv()

        @pl.loop(lo, hi)
        def _(m):
            ss[dx, m] = (ss[dx, m].astype(F32) + got[dx, m].astype(F32)).astype(BF16)

    def to_owner(dx, k, at):
        rel = PLANE[k]
        block = pl.ds(pl.multiple_of((y + rel[1]) % 4 * 64 + (zl + rel[3]) % 2 * 32, 32), 32)
        return send(ss.at[dx, at, block, :], red.at[dx, k, at], rel)

    def launch(dx, lo, hi):
        mid = (lo + hi) // 2
        low, high = pl.ds(lo, mid - lo), pl.ds(mid, hi - mid)
        up = send(ss.at[dx, low, y_rows(2), :], via.at[dx, low], y_by(1))
        down = send(ss.at[dx, high, y_rows(2), :], via.at[dx, high], y_by(-1))
        sent = [to_owner(dx, 0, high), to_owner(dx, 1, low), to_owner(dx, 2, high), to_owner(dx, 3, low),
                to_owner(dx, 4, pl.ds(lo, hi - lo))]
        return up, down, sent

    def pass_on(dx, lo, hi, started):
        mid = (lo + hi) // 2
        sent = started[2]
        for part, d, first, last in ((0, 1, lo, mid), (1, 3, mid, hi)):
            started[part].wait_recv()
            for m in range(first, last):
                at = (dx, m, y_rows(d), slice(None))
                ss[at] = (ss[at].astype(F32) + via[dx, m].astype(F32)).astype(BF16)
            at = pl.ds(first, last - first)
            sent += [to_owner(dx, part, at), to_owner(dx, part + 2, at)]
        return sent

    partial(0, 0, 2)
    started0 = launch(0, 0, 2)
    partial(0, 2, 4)
    r0 = pass_on(0, 0, 2, started0)
    forwards = []
    for part in range(2):
        c_pairs[part][0].wait_recv()
        a = send(ctx.at[3, part, pl.ds(0, 2)], ctx.at[2, part, pl.ds(0, 2)], x_by(1))
        c_pairs[part][1].wait_recv()
        b = send(ctx.at[1, part, pl.ds(2, 2)], ctx.at[2, part, pl.ds(2, 2)], x_by(-1))
        forwards += [a, b]
    partial(1, 0, 4)
    started1 = launch(1, 0, 4)
    partial(3, 0, 4)
    started3 = launch(3, 0, 4)
    r1 = pass_on(1, 0, 4, started1)
    r3 = pass_on(3, 0, 4, started3)
    for copy in forwards:
        copy.wait_recv()
    partial(2, 0, 4)
    r2 = pass_on(2, 0, 4, launch(2, 0, 4))
    r0 += pass_on(0, 2, 4, launch(0, 2, 4))

    own_block = pl.ds(pl.multiple_of(group * 32, 32), 32)
    back = []
    for dx, sent in ((1, r1), (3, r3), (2, r2), (0, r0)):
        for copy in sent:
            copy.wait_recv()

        @pl.loop(0, 4)
        def _(m):
            total = ss[dx, m, own_block, :].astype(F32)
            for k in range(len(PLANE)):
                total += red[dx, k, m].astype(F32)
            if dx == 0:
                parts[m] = total.astype(BF16)
            else:
                fin[dx, m] = total.astype(BF16)
        if dx != 0:
            back.append(send(fin.at[dx], parts.at[pl.ds((4 - dx) % 4 * 4, 4)], x_by(dx)))
    for copy in back:
        copy.wait_recv()

    out[...] = parts[...]
    for copy in copies:
        copy.wait_send()


def place(held, parts, out):
    rep = lax.axis_index("rep")
    for r in range(16):
        slot = (r // 4 + 4 - rep // 4) % 4 * 4 + (r % 4 + 4 - rep % 4) % 4
        out[:, pl.ds(pl.multiple_of(held[r] * SL, SL), SL)] = parts[slot]


N_COPIES = 30 + 15 + 4 + 1 + 8 + 5 * 12 + 3


def tables():
    p = np.arange(SEQ)
    where_at = (p // 128 * 128 + p // 32 % 2 * 64 + p // 64 % 2 * 32 + p % 32).astype(np.float32)
    freqs = np.float32(ROPE_THETA) ** (-(np.arange(HD // 2, dtype=np.float32) * np.float32(2.0)) / np.float32(HD))
    angles = where_at[:, None] * freqs[None, :]
    cosine, sine = np.cos(angles), np.sin(angles)
    return (np.concatenate([cosine, cosine], 1).astype(np.float32),
            np.concatenate([-sine, sine], 1).astype(np.float32))


def per_device(hidden, norm_gain, q_weight, kv_weight, out_weight, held_slice):
    cosine, sine = tables()
    vm = pltpu.VMEM
    parts = pl.pallas_call(
        kernel,
        out_shape=jax.ShapeDtypeStruct((16, 32, SL), BF16),
        in_specs=[pl.BlockSpec(memory_space=pltpu.SMEM)] + [pl.BlockSpec(memory_space=pl.ANY)] * 7,
        out_specs=pl.BlockSpec(memory_space=pltpu.VMEM),
        scratch_shapes=[
            vm((32, D), BF16), vm((D // HD, HD), BF16), vm((SEQ, HD), F32), vm((SEQ, HD), F32),
            vm((16, SEQ, SL), BF16), vm((16, SL, WC), BF16), vm((4, SL, SL), BF16), vm((SEQ, WC), F32),
            vm((2, SEQ, HD), BF16), vm((4, SEQ, HD), BF16), vm((4, 2, 4, 2, 64, 256), BF16),
            vm((4, 4, 256, SL), BF16), vm((4, 4, 256, SL), BF16), vm((4, 4, 256, SL), BF16),
            vm((4, 4, 64, SL), BF16), vm((4, 5, 4, 32, SL), BF16), vm((4, 4, 32, SL), BF16), vm((16, 32, SL), BF16),
            pltpu.SemaphoreType.DMA((7,)), pltpu.SemaphoreType.DMA((N_COPIES,)), pltpu.SemaphoreType.DMA((N_COPIES,)),
        ],
        compiler_params=pltpu.CompilerParams(
            collective_id=0, has_side_effects=True, vmem_limit_bytes=62 * 1024 * 1024),
        name="block",
    )(held_slice, hidden, norm_gain.reshape(D // HD, HD), q_weight, kv_weight, out_weight,
      jnp.asarray(cosine), jnp.asarray(sine))
    return pl.pallas_call(
        place,
        out_shape=jax.ShapeDtypeStruct((32, D), BF16),
        in_specs=[pl.BlockSpec(memory_space=pltpu.SMEM), pl.BlockSpec(memory_space=pltpu.VMEM)],
        out_specs=pl.BlockSpec(memory_space=pltpu.VMEM),
        name="place",
    )(held_slice, parts)


def solution(mesh):
    return jax.shard_map(
        per_device,
        mesh=mesh,
        in_specs=(P(("rep", "tp"), None), P(), P("rep", "tp"), P("rep", None), P("tp", "rep"), P()),
        out_specs=P(("rep", "tp"), None),
        check_vma=False,
    )
```

```python
import jax
import jax.numpy as jnp
import numpy as np
from jax import lax
from jax.experimental import pallas as pl
from jax.experimental.pallas import tpu as pltpu
from jax.sharding import PartitionSpec as P

HD = 128
HQ = 64
KVH = 8
D = 8192
SEQ = 512
SL = 512
WC = 640
ROPE_THETA = 500000.0
MESH = pl.DeviceIdType.MESH
F32, BF16 = jnp.float32, jnp.bfloat16

CORE = (0, 0, 0, 0, 1)
ZL = (0, 0, 0, 1, 0)
PLANE = [(0, 1, 0, 0, 0), (0, 3, 0, 0, 0), (0, 1, 0, 1, 0), (0, 3, 0, 1, 0), ZL]


def x_by(d):
    return (d % 4, 0, 0, 0, 0)


def z_by(d):
    return (0, 0, d % 4, 0, 0)


def y_by(d):
    return (0, d % 4, 0, 0, 0)


PEERS = [x_by(1), x_by(2), x_by(3), z_by(1), z_by(3), y_by(2), CORE] + PLANE


def kernel(held, hidden, gain, q_weight, kv_weight, out_weight, cos_hbm, sin_hbm, out,
           hid, gn, cos, sin, tok, w, wo, acc, kv, q, ctx, give, got, ss, via, red, fin, parts, lsem, ssem, rsem):
    rep, tp = lax.axis_index("rep"), lax.axis_index("tp")
    x, zh = rep // 4, rep % 4
    y, zl, c = tp // 4, (tp // 2) % 2, tp % 2

    def target(rel):
        dx, dy, dz, dl, dc = rel
        return (
            (x + dx) % 4 * 4 + (zh + dz) % 4,
            (y + dy) % 4 * 4 + (zl + dl) % 2 * 2 + (c + dc) % 2,
        )

    copies = []

    def send(src, dst, rel):
        k = len(copies)
        copy = pltpu.make_async_remote_copy(
            src_ref=src, dst_ref=dst, send_sem=ssem.at[k], recv_sem=rsem.at[k],
            device_id=target(rel), device_id_type=MESH)
        copy.start()
        copies.append(copy)
        return copy

    group = y * 2 + zl
    locals_ = [
        pltpu.make_async_copy(q_weight, w.at[0, :, pl.ds(0, SL)], lsem.at[0]),
        pltpu.make_async_copy(
            kv_weight.at[:, pl.ds(pl.multiple_of(c * KVH * HD + group * HD, HD), HD)],
            w.at[0, :, pl.ds(SL, HD)], lsem.at[1]),
        pltpu.make_async_copy(hidden, hid, lsem.at[2]),
        pltpu.make_async_copy(gain, gn, lsem.at[3]),
        pltpu.make_async_copy(out_weight, wo.at[0], lsem.at[4]),
        pltpu.make_async_copy(cos_hbm, cos, lsem.at[5]),
        pltpu.make_async_copy(sin_hbm, sin, lsem.at[6]),
    ]
    for copy in locals_:
        copy.start()

    barrier = pltpu.get_barrier_semaphore()
    for rel in PEERS:
        pl.semaphore_signal(barrier, inc=1, device_id=target(rel), device_id_type=MESH)
    pl.semaphore_wait(barrier, len(PEERS))

    def half(dx, dz, part):
        return w.at[dx % 4 * 4 + dz % 4, pl.ds(part * (SL // 2), SL // 2), :]

    def x_send(dz, part, d):
        return send(half(0, dz, part), half(-d, dz, part), x_by(d))

    def x_forward(copy, dz, part):
        copy.wait_recv()
        d = 1 - 2 * part
        return send(half(-d, dz, part), half(-2 * d, dz, part), x_by(d))

    locals_[0].wait()
    locals_[1].wait()
    z_first = send(half(0, 0, 0), half(0, -1, 0), z_by(1)), send(half(0, 0, 1), half(0, 1, 1), z_by(-1))
    xs = {}
    for part in range(2):
        xs[0, part, 1] = x_send(0, part, 1)
        xs[0, 1 - part, -1] = x_send(0, 1 - part, -1)

    z_second = send(half(0, 0, 1), half(0, -1, 1), z_by(1)), send(half(0, 0, 0), half(0, 1, 0), z_by(-1))

    def rows(dy, dl, dc=0):
        return pl.ds(pl.multiple_of((y + dy) % 4 * 128 + (c + dc) % 2 * 64 + (zl + dl) % 2 * 32, 32), 32)

    locals_[2].wait()
    locals_[3].wait()
    states = hid[...].astype(F32)
    factor = lax.rsqrt(jnp.mean(states * states, axis=-1, keepdims=True) + 1e-05)
    for n in range(D // HD):
        one = hid[:, n * HD:(n + 1) * HD].astype(F32) * factor * gn[n:n + 1, :].astype(F32)
        tok[n // 4, rows(0, 0), n % 4 * HD:(n % 4 + 1) * HD] = one.astype(BF16)

    def tok_at(dy, dl):
        return tok.at[:, rows(dy, dl), :]

    t_z = send(tok_at(0, 0), tok_at(0, 0), ZL)
    t_y0 = [send(tok_at(0, 0), tok_at(0, 0), y_by(d)) for d in (1, 3, 2)]
    t_core = [send(tok_at(0, 0), tok_at(0, 0), CORE)]

    ends = [(0, x_forward(xs[0, 0, 1], 0, 0), x_forward(xs[0, 1, -1], 0, 1))]
    z_first[0].wait_recv()
    zf0 = send(half(0, -1, 0), half(0, -2, 0), z_by(1))
    for d in (1, -1):
        xs[-1, 0, d] = x_send(-1, 0, d)
    z_first[1].wait_recv()
    zf1 = send(half(0, 1, 1), half(0, 2, 1), z_by(-1))
    for d in (-1, 1):
        xs[1, 1, d] = x_send(1, 1, d)
    z_second[0].wait_recv()
    for d in (-1, 1):
        xs[-1, 1, d] = x_send(-1, 1, d)
    z_second[1].wait_recv()
    for d in (1, -1):
        xs[1, 0, d] = x_send(1, 0, d)
    f30 = x_forward(xs[-1, 0, 1], -1, 0)
    f11 = x_forward(xs[1, 1, -1], 1, 1)
    for d, copy in zip((1, 3, 2), t_y0):
        copy.wait_recv()
        t_core.append(send(tok_at(-d, 0), tok_at(-d, 0), CORE))
    t_z.wait_recv()
    t_y1 = [send(tok_at(0, 1), tok_at(0, 1), y_by(d)) for d in (1, 3, 2)]
    t_core.append(send(tok_at(0, 1), tok_at(0, 1), CORE))
    zf0.wait_recv()
    for d in (1, -1):
        xs[2, 0, d] = x_send(2, 0, d)
    zf1.wait_recv()
    for d in (-1, 1):
        xs[2, 1, d] = x_send(2, 1, d)
    locals_[4].wait()
    wo_pair = send(wo.at[0], wo.at[3], z_by(1)), send(wo.at[0], wo.at[1], z_by(-1))
    ends.append((-1, f30, x_forward(xs[-1, 1, -1], -1, 1)))
    ends.append((1, x_forward(xs[1, 0, 1], 1, 0), f11))
    for d, copy in zip((1, 3, 2), t_y1):
        copy.wait_recv()
        t_core.append(send(tok_at(-d, 1), tok_at(-d, 1), CORE))
    for copy in t_core:
        copy.wait_recv()

    acc[...] = jnp.zeros_like(acc)

    def project(dx, dz):
        source = held[(x + dx) % 4 * 4 + (zh + dz) % 4]
        slot = dx % 4 * 4 + dz % 4

        @pl.loop(0, 2)
        def _(i):
            at = pl.ds(pl.multiple_of(i * 256, 256), 256)
            acc[at, :] += jnp.dot(tok[source, at, :], w[slot], preferred_element_type=F32)

    for dz in (0, -1, 1, 2):
        project(0, dz)
    for dz in (0, -1, 1):
        xs[dz, 1, 1].wait_recv()
        project(-1, dz)
        xs[dz, 0, -1].wait_recv()
        project(1, dz)
    ends.append((2, x_forward(xs[2, 0, 1], 2, 0), x_forward(xs[2, 1, -1], 2, 1)))
    wo_pair[0].wait_recv()
    wf0 = send(wo.at[3, pl.ds(0, 256), :], wo.at[2, pl.ds(0, 256), :], z_by(1))
    wo_pair[1].wait_recv()
    wf1 = send(wo.at[1, pl.ds(256, 256), :], wo.at[2, pl.ds(256, 256), :], z_by(-1))
    xs[2, 1, 1].wait_recv()
    project(-1, 2)
    xs[2, 0, -1].wait_recv()
    project(1, 2)
    for dz, a, b in ends:
        a.wait_recv()
        b.wait_recv()
        project(2, dz)

    locals_[5].wait()
    locals_[6].wait()
    pair_own = acc[:, SL:WC]
    turned = pair_own * cos[...] + pltpu.roll(pair_own, HD // 2, 1) * sin[...]
    kv[c] = jnp.where(c == 0, turned, pair_own).astype(BF16)
    kv_copy = send(kv.at[c], kv.at[c], CORE)
    for n in range(4):
        one = acc[:, n * HD:(n + 1) * HD]
        q[n] = (one * cos[...] + pltpu.roll(one, HD // 2, 1) * sin[...]).astype(BF16)
    kv_copy.wait_recv()

    def position(p):
        return p // 32 % 2 * 64 + p // 64 * 32 + p % 32

    earlier = (position(lax.broadcasted_iota(jnp.int32, (HD, 1), 0))
               >= position(lax.broadcasted_iota(jnp.int32, (1, HD), 1)))
    scale = HD**-0.5 / np.log(2.0)

    def heads(part):
        for n in range(2):
            for b in range(4):
                end = (b + 1) * 128
                scores = lax.dot_general(
                    q[part * 2 + n, b * 128:end, :], kv[0, :end, :], (((1,), (1,)), ((), ())),
                    preferred_element_type=F32)
                near = jnp.where(earlier, scores[:, end - 128:], -1e30)
                scores = jnp.concatenate([scores[:, :end - 128], near], axis=1) if b else near
                weights = jnp.exp2((scores - jnp.max(scores, axis=-1, keepdims=True)) * scale)
                probs = (weights * (1.0 / jnp.sum(weights, axis=-1, keepdims=True))).astype(BF16)
                mixed = jnp.dot(probs, kv[1, :end, :], preferred_element_type=F32).astype(BF16)
                ctx[0, part, b, :, :, n * HD:(n + 1) * HD] = mixed.reshape(2, 64, HD)

    c_pairs = []
    for part in range(2):
        heads(part)
        c_pairs.append((send(ctx.at[0, part], ctx.at[3, part], x_by(1)),
                        send(ctx.at[0, part], ctx.at[1, part], x_by(-1))))
    wf0.wait_recv()
    wf1.wait_recv()

    def product(dx, core, m):
        first, second = (ctx[dx, part, :, core].reshape(256, 256) for part in range(2))
        return (jnp.dot(first, wo[m, pl.ds(0, 256), :], preferred_element_type=F32)
                + jnp.dot(second, wo[m, pl.ds(256, 256), :], preferred_element_type=F32)).astype(BF16)

    def y_rows(d):
        return pl.ds(pl.multiple_of((y + d) % 4 * 64, 64), 64)

    def partial(dx, lo, hi):
        @pl.loop(lo, hi)
        def _(m):
            give[dx, m] = product(dx, 1 - c, m)
        at = pl.ds(lo, hi - lo)
        swap = send(give.at[dx, at], got.at[dx, at], CORE)

        @pl.loop(lo, hi)
        def _(m):
            ss[dx, m] = product(dx, c, m)
        swap.wait_recv()

        @pl.loop(lo, hi)
        def _(m):
            ss[dx, m] = (ss[dx, m].astype(F32) + got[dx, m].astype(F32)).astype(BF16)

    def to_owner(dx, k, at):
        rel = PLANE[k]
        block = pl.ds(pl.multiple_of((y + rel[1]) % 4 * 64 + (zl + rel[3]) % 2 * 32, 32), 32)
        return send(ss.at[dx, at, block, :], red.at[dx, k, at], rel)

    def launch(dx, lo, hi):
        mid = (lo + hi) // 2
        low, high = pl.ds(lo, mid - lo), pl.ds(mid, hi - mid)
        up = send(ss.at[dx, low, y_rows(2), :], via.at[dx, low], y_by(1))
        down = send(ss.at[dx, high, y_rows(2), :], via.at[dx, high], y_by(-1))
        sent = [to_owner(dx, 0, high), to_owner(dx, 1, low), to_owner(dx, 2, high), to_owner(dx, 3, low),
                to_owner(dx, 4, pl.ds(lo, hi - lo))]
        return up, down, sent

    def pass_on(dx, lo, hi, started):
        mid = (lo + hi) // 2
        sent = started[2]
        for part, d, first, last in ((0, 1, lo, mid), (1, 3, mid, hi)):
            started[part].wait_recv()
            for m in range(first, last):
                at = (dx, m, y_rows(d), slice(None))
                ss[at] = (ss[at].astype(F32) + via[dx, m].astype(F32)).astype(BF16)
            at = pl.ds(first, last - first)
            sent += [to_owner(dx, part, at), to_owner(dx, part + 2, at)]
        return sent

    partial(0, 0, 2)
    started0 = launch(0, 0, 2)
    partial(0, 2, 4)
    started00 = launch(0, 2, 4)
    r0 = pass_on(0, 0, 2, started0) + pass_on(0, 2, 4, started00)
    forwards = []
    for part in range(2):
        c_pairs[part][0].wait_recv()
        a = send(ctx.at[3, part, pl.ds(0, 2)], ctx.at[2, part, pl.ds(0, 2)], x_by(1))
        c_pairs[part][1].wait_recv()
        b = send(ctx.at[1, part, pl.ds(2, 2)], ctx.at[2, part, pl.ds(2, 2)], x_by(-1))
        forwards += [a, b]
    partial(1, 0, 4)
    started1 = launch(1, 0, 4)
    partial(3, 0, 4)
    started3 = launch(3, 0, 4)
    r1 = pass_on(1, 0, 4, started1)
    for copy in forwards:
        copy.wait_recv()
    partial(2, 0, 4)
    started2 = launch(2, 0, 4)
    r3 = pass_on(3, 0, 4, started3)
    r2 = pass_on(2, 0, 4, started2)

    own_block = pl.ds(pl.multiple_of(group * 32, 32), 32)
    back = []
    for dx, sent in ((0, r0), (1, r1), (3, r3), (2, r2)):
        for copy in sent:
            copy.wait_recv()

        @pl.loop(0, 4)
        def _(m):
            total = ss[dx, m, own_block, :].astype(F32)
            for k in range(len(PLANE)):
                total += red[dx, k, m].astype(F32)
            if dx == 0:
                parts[m] = total.astype(BF16)
            else:
                fin[dx, m] = total.astype(BF16)
        if dx != 0:
            back.append(send(fin.at[dx], parts.at[pl.ds((4 - dx) % 4 * 4, 4)], x_by(dx)))
    for copy in back:
        copy.wait_recv()

    out[...] = parts[...]
    for copy in copies:
        copy.wait_send()


def place(held, parts, out):
    rep = lax.axis_index("rep")
    for r in range(16):
        slot = (r // 4 + 4 - rep // 4) % 4 * 4 + (r % 4 + 4 - rep % 4) % 4
        out[:, pl.ds(pl.multiple_of(held[r] * SL, SL), SL)] = parts[slot]


N_COPIES = 30 + 15 + 4 + 1 + 8 + 5 * 12 + 3


def tables():
    p = np.arange(SEQ)
    where_at = (p // 128 * 128 + p // 32 % 2 * 64 + p // 64 % 2 * 32 + p % 32).astype(np.float32)
    freqs = np.float32(ROPE_THETA) ** (-(np.arange(HD // 2, dtype=np.float32) * np.float32(2.0)) / np.float32(HD))
    angles = where_at[:, None] * freqs[None, :]
    cosine, sine = np.cos(angles), np.sin(angles)
    return (np.concatenate([cosine, cosine], 1).astype(np.float32),
            np.concatenate([-sine, sine], 1).astype(np.float32))


def per_device(hidden, norm_gain, q_weight, kv_weight, out_weight, held_slice):
    cosine, sine = tables()
    vm = pltpu.VMEM
    parts = pl.pallas_call(
        kernel,
        out_shape=jax.ShapeDtypeStruct((16, 32, SL), BF16),
        in_specs=[pl.BlockSpec(memory_space=pltpu.SMEM)] + [pl.BlockSpec(memory_space=pl.ANY)] * 7,
        out_specs=pl.BlockSpec(memory_space=pltpu.VMEM),
        scratch_shapes=[
            vm((32, D), BF16), vm((D // HD, HD), BF16), vm((SEQ, HD), F32), vm((SEQ, HD), F32),
            vm((16, SEQ, SL), BF16), vm((16, SL, WC), BF16), vm((4, SL, SL), BF16), vm((SEQ, WC), F32),
            vm((2, SEQ, HD), BF16), vm((4, SEQ, HD), BF16), vm((4, 2, 4, 2, 64, 256), BF16),
            vm((4, 4, 256, SL), BF16), vm((4, 4, 256, SL), BF16), vm((4, 4, 256, SL), BF16),
            vm((4, 4, 64, SL), BF16), vm((4, 5, 4, 32, SL), BF16), vm((4, 4, 32, SL), BF16), vm((16, 32, SL), BF16),
            pltpu.SemaphoreType.DMA((7,)), pltpu.SemaphoreType.DMA((N_COPIES,)), pltpu.SemaphoreType.DMA((N_COPIES,)),
        ],
        compiler_params=pltpu.CompilerParams(
            collective_id=0, has_side_effects=True, vmem_limit_bytes=62 * 1024 * 1024),
        name="block",
    )(held_slice, hidden, norm_gain.reshape(D // HD, HD), q_weight, kv_weight, out_weight,
      jnp.asarray(cosine), jnp.asarray(sine))
    return pl.pallas_call(
        place,
        out_shape=jax.ShapeDtypeStruct((32, D), BF16),
        in_specs=[pl.BlockSpec(memory_space=pltpu.SMEM), pl.BlockSpec(memory_space=pltpu.VMEM)],
        out_specs=pl.BlockSpec(memory_space=pltpu.VMEM),
        name="place",
    )(held_slice, parts)


def solution(mesh):
    return jax.shard_map(
        per_device,
        mesh=mesh,
        in_specs=(P(("rep", "tp"), None), P(), P("rep", "tp"), P("rep", None), P("tp", "rep"), P()),
        out_specs=P(("rep", "tp"), None),
        check_vma=False,
    )
```

```python
import jax
import jax.numpy as jnp
import numpy as np
from jax import lax
from jax.experimental import pallas as pl
from jax.experimental.pallas import tpu as pltpu
from jax.sharding import PartitionSpec as P

HD = 128
HQ = 64
KVH = 8
D = 8192
SEQ = 512
SL = 512
REST = 32
HALF = (SL - REST) // 2
WC = 640
ROPE_THETA = 500000.0
MESH = pl.DeviceIdType.MESH
F32, BF16 = jnp.float32, jnp.bfloat16

CORE = (0, 0, 0, 0, 1)
ZL = (0, 0, 0, 1, 0)
PLANE = [(0, 1, 0, 0, 0), (0, 3, 0, 0, 0), (0, 1, 0, 1, 0), (0, 3, 0, 1, 0), ZL]


def x_by(d):
    return (d % 4, 0, 0, 0, 0)


def z_by(d):
    return (0, 0, d % 4, 0, 0)


def y_by(d):
    return (0, d % 4, 0, 0, 0)


PEERS = [x_by(1), x_by(2), x_by(3), z_by(1), z_by(3), y_by(2), CORE] + PLANE


def kernel(held, hidden, gain, q_weight, kv_weight, out_weight, cos_hbm, sin_hbm, out,
           hid, gn, cos, sin, tok, w, wo, acc, kv, q, ctx, give, got, ss, via, red, fin, parts, lsem, ssem, rsem):
    rep, tp = lax.axis_index("rep"), lax.axis_index("tp")
    x, zh = rep // 4, rep % 4
    y, zl, c = tp // 4, (tp // 2) % 2, tp % 2

    def target(rel):
        dx, dy, dz, dl, dc = rel
        return (
            (x + dx) % 4 * 4 + (zh + dz) % 4,
            (y + dy) % 4 * 4 + (zl + dl) % 2 * 2 + (c + dc) % 2,
        )

    copies = []

    def send(src, dst, rel):
        k = len(copies)
        copy = pltpu.make_async_remote_copy(
            src_ref=src, dst_ref=dst, send_sem=ssem.at[k], recv_sem=rsem.at[k],
            device_id=target(rel), device_id_type=MESH)
        copy.start()
        copies.append(copy)
        return copy

    group = y * 2 + zl
    locals_ = [
        pltpu.make_async_copy(q_weight, w.at[0, 0, :, pl.ds(0, SL)], lsem.at[0]),
        pltpu.make_async_copy(
            kv_weight.at[:, pl.ds(pl.multiple_of(c * KVH * HD + group * HD, HD), HD)],
            w.at[0, 0, :, pl.ds(SL, HD)], lsem.at[1]),
        pltpu.make_async_copy(hidden, hid, lsem.at[2]),
        pltpu.make_async_copy(gain, gn, lsem.at[3]),
        pltpu.make_async_copy(out_weight, wo.at[0], lsem.at[4]),
        pltpu.make_async_copy(cos_hbm, cos, lsem.at[5]),
        pltpu.make_async_copy(sin_hbm, sin, lsem.at[6]),
    ]
    for copy in locals_:
        copy.start()

    barrier = pltpu.get_barrier_semaphore()
    for rel in PEERS:
        pl.semaphore_signal(barrier, inc=1, device_id=target(rel), device_id_type=MESH)
    pl.semaphore_wait(barrier, len(PEERS))

    def half(dx, dz, part):
        return w.at[dx % 4, dz % 4, pl.ds(part * HALF, HALF), :]

    def rest(dx, lo=0, n=REST):
        return w.at[dx % 4, 0, pl.ds(2 * HALF + lo, n), :]

    def rests(dz, lo=0, n=4):
        return w.at[pl.ds(lo, n), dz % 4, pl.ds(2 * HALF, REST), :]

    def x_send(dz, part, d):
        return send(half(0, dz, part), half(-d, dz, part), x_by(d))

    def x_forward(copy, dz, part):
        copy.wait_recv()
        d = 1 - 2 * part
        return send(half(-d, dz, part), half(-2 * d, dz, part), x_by(d))

    locals_[0].wait()
    locals_[1].wait()
    z_first = send(half(0, 0, 0), half(0, -1, 0), z_by(1)), send(half(0, 0, 1), half(0, 1, 1), z_by(-1))
    rest_x = send(rest(0), rest(-1), x_by(1)), send(rest(0), rest(1), x_by(-1))
    xs = {}
    for part in range(2):
        xs[0, part, 1] = x_send(0, part, 1)
        xs[0, 1 - part, -1] = x_send(0, 1 - part, -1)

    z_second = send(half(0, 0, 1), half(0, -1, 1), z_by(1)), send(half(0, 0, 0), half(0, 1, 0), z_by(-1))

    def rows(dy, dl, dc=0):
        return pl.ds(pl.multiple_of((y + dy) % 4 * 128 + (c + dc) % 2 * 64 + (zl + dl) % 2 * 32, 32), 32)

    locals_[2].wait()
    locals_[3].wait()
    states = hid[...].astype(F32)
    factor = lax.rsqrt(jnp.mean(states * states, axis=-1, keepdims=True) + 1e-05)
    for n in range(D // HD):
        one = hid[:, n * HD:(n + 1) * HD].astype(F32) * factor * gn[n:n + 1, :].astype(F32)
        tok[n // 4, rows(0, 0), n % 4 * HD:(n % 4 + 1) * HD] = one.astype(BF16)

    def tok_at(dy, dl):
        return tok.at[:, rows(dy, dl), :]

    t_z = send(tok_at(0, 0), tok_at(0, 0), ZL)
    t_y0 = [send(tok_at(0, 0), tok_at(0, 0), y_by(d)) for d in (1, 3, 2)]
    t_core = [send(tok_at(0, 0), tok_at(0, 0), CORE)]

    rest_x[0].wait_recv()
    rest_xf0 = send(rest(-1, 0, REST // 2), rest(-2, 0, REST // 2), x_by(1))
    rest_x[1].wait_recv()
    rest_xf1 = send(rest(1, REST // 2, REST // 2), rest(2, REST // 2, REST // 2), x_by(-1))
    ends = [(0, x_forward(xs[0, 0, 1], 0, 0), x_forward(xs[0, 1, -1], 0, 1))]
    z_first[0].wait_recv()
    zf0 = send(half(0, -1, 0), half(0, -2, 0), z_by(1))
    for d in (1, -1):
        xs[-1, 0, d] = x_send(-1, 0, d)
    z_first[1].wait_recv()
    zf1 = send(half(0, 1, 1), half(0, 2, 1), z_by(-1))
    for d in (-1, 1):
        xs[1, 1, d] = x_send(1, 1, d)
    rest_xf0.wait_recv()
    rest_xf1.wait_recv()
    rest_z = send(rests(0), rests(-1), z_by(1)), send(rests(0), rests(1), z_by(-1))
    z_second[0].wait_recv()
    for d in (-1, 1):
        xs[-1, 1, d] = x_send(-1, 1, d)
    z_second[1].wait_recv()
    for d in (1, -1):
        xs[1, 0, d] = x_send(1, 0, d)
    f30 = x_forward(xs[-1, 0, 1], -1, 0)
    f11 = x_forward(xs[1, 1, -1], 1, 1)
    for d, copy in zip((1, 3, 2), t_y0):
        copy.wait_recv()
        t_core.append(send(tok_at(-d, 0), tok_at(-d, 0), CORE))
    t_z.wait_recv()
    t_y1 = [send(tok_at(0, 1), tok_at(0, 1), y_by(d)) for d in (1, 3, 2)]
    t_core.append(send(tok_at(0, 1), tok_at(0, 1), CORE))
    zf0.wait_recv()
    for d in (1, -1):
        xs[2, 0, d] = x_send(2, 0, d)
    zf1.wait_recv()
    for d in (-1, 1):
        xs[2, 1, d] = x_send(2, 1, d)
    ends.append((-1, f30, x_forward(xs[-1, 1, -1], -1, 1)))
    ends.append((1, x_forward(xs[1, 0, 1], 1, 0), f11))
    rest_z[0].wait_recv()
    rest_zf0 = send(rests(-1, 0, 2), rests(2, 0, 2), z_by(1))
    rest_z[1].wait_recv()
    rest_zf1 = send(rests(1, 2, 2), rests(2, 2, 2), z_by(-1))
    locals_[4].wait()
    wo_pair = send(wo.at[0], wo.at[3], z_by(1)), send(wo.at[0], wo.at[1], z_by(-1))
    for d, copy in zip((1, 3, 2), t_y1):
        copy.wait_recv()
        t_core.append(send(tok_at(-d, 1), tok_at(-d, 1), CORE))
    for copy in t_core:
        copy.wait_recv()

    acc[...] = jnp.zeros_like(acc)

    def project(dx, dz):
        source = held[(x + dx) % 4 * 4 + (zh + dz) % 4]

        @pl.loop(0, 2)
        def _(i):
            at = pl.ds(pl.multiple_of(i * 256, 256), 256)
            acc[at, :] += jnp.dot(tok[source, at, :], w[dx % 4, dz % 4], preferred_element_type=F32)

    for dz in (0, -1, 1):
        project(0, dz)
    for dz in (0, -1, 1):
        xs[dz, 1, 1].wait_recv()
        project(-1, dz)
        xs[dz, 0, -1].wait_recv()
        project(1, dz)
    ends.append((2, x_forward(xs[2, 0, 1], 2, 0), x_forward(xs[2, 1, -1], 2, 1)))
    rest_zf0.wait_recv()
    rest_zf1.wait_recv()
    project(0, 2)
    xs[2, 1, 1].wait_recv()
    project(-1, 2)
    xs[2, 0, -1].wait_recv()
    project(1, 2)
    for dz, a, b in ends:
        a.wait_recv()
        b.wait_recv()
        project(2, dz)

    locals_[5].wait()
    locals_[6].wait()
    pair_own = acc[:, SL:WC]
    turned = pair_own * cos[...] + pltpu.roll(pair_own, HD // 2, 1) * sin[...]
    kv[c] = jnp.where(c == 0, turned, pair_own).astype(BF16)
    kv_copy = send(kv.at[c], kv.at[c], CORE)
    wo_pair[0].wait_recv()
    wf0 = send(wo.at[3, pl.ds(0, 256), :], wo.at[2, pl.ds(0, 256), :], z_by(1))
    wo_pair[1].wait_recv()
    wf1 = send(wo.at[1, pl.ds(256, 256), :], wo.at[2, pl.ds(256, 256), :], z_by(-1))
    for n in range(4):
        one = acc[:, n * HD:(n + 1) * HD]
        q[n] = (one * cos[...] + pltpu.roll(one, HD // 2, 1) * sin[...]).astype(BF16)
    kv_copy.wait_recv()

    def position(p):
        return p // 32 % 2 * 64 + p // 64 * 32 + p % 32

    earlier = (position(lax.broadcasted_iota(jnp.int32, (HD, 1), 0))
               >= position(lax.broadcasted_iota(jnp.int32, (1, HD), 1)))
    scale = HD**-0.5 / np.log(2.0)

    def heads(part):
        for n in range(2):
            for b in range(4):
                end = (b + 1) * 128
                scores = lax.dot_general(
                    q[part * 2 + n, b * 128:end, :], kv[0, :end, :], (((1,), (1,)), ((), ())),
                    preferred_element_type=F32)
                near = jnp.where(earlier, scores[:, end - 128:], -1e30)
                scores = jnp.concatenate([scores[:, :end - 128], near], axis=1) if b else near
                weights = jnp.exp2((scores - jnp.max(scores, axis=-1, keepdims=True)) * scale)
                probs = (weights * (1.0 / jnp.sum(weights, axis=-1, keepdims=True))).astype(BF16)
                mixed = jnp.dot(probs, kv[1, :end, :], preferred_element_type=F32).astype(BF16)
                ctx[0, part, b, :, :, n * HD:(n + 1) * HD] = mixed.reshape(2, 64, HD)

    c_pairs = []
    for part in range(2):
        heads(part)
        c_pairs.append((send(ctx.at[0, part], ctx.at[3, part], x_by(1)),
                        send(ctx.at[0, part], ctx.at[1, part], x_by(-1))))

    def product(dx, core, m):
        first, second = (ctx[dx, part, :, core].reshape(256, 256) for part in range(2))
        return (jnp.dot(first, wo[m, pl.ds(0, 256), :], preferred_element_type=F32)
                + jnp.dot(second, wo[m, pl.ds(256, 256), :], preferred_element_type=F32)).astype(BF16)

    def y_rows(d):
        return pl.ds(pl.multiple_of((y + d) % 4 * 64, 64), 64)

    def partial(dx, lo, hi):
        @pl.loop(lo, hi)
        def _(m):
            give[dx, m] = product(dx, 1 - c, m)
        at = pl.ds(lo, hi - lo)
        swap = send(give.at[dx, at], got.at[dx, at], CORE)

        @pl.loop(lo, hi)
        def _(m):
            ss[dx, m] = product(dx, c, m)
        swap.wait_recv()

        @pl.loop(lo, hi)
        def _(m):
            ss[dx, m] = (ss[dx, m].astype(F32) + got[dx, m].astype(F32)).astype(BF16)

    def to_owner(dx, k, at):
        rel = PLANE[k]
        block = pl.ds(pl.multiple_of((y + rel[1]) % 4 * 64 + (zl + rel[3]) % 2 * 32, 32), 32)
        return send(ss.at[dx, at, block, :], red.at[dx, k, at], rel)

    def launch(dx, lo, hi):
        mid = (lo + hi) // 2
        low, high = pl.ds(lo, mid - lo), pl.ds(mid, hi - mid)
        up = send(ss.at[dx, low, y_rows(2), :], via.at[dx, low], y_by(1))
        down = send(ss.at[dx, high, y_rows(2), :], via.at[dx, high], y_by(-1))
        sent = [to_owner(dx, 0, high), to_owner(dx, 1, low), to_owner(dx, 2, high), to_owner(dx, 3, low),
                to_owner(dx, 4, pl.ds(lo, hi - lo))]
        return up, down, sent

    def pass_on(dx, lo, hi, started):
        mid = (lo + hi) // 2
        sent = started[2]
        for part, d, first, last in ((0, 1, lo, mid), (1, 3, mid, hi)):
            started[part].wait_recv()
            for m in range(first, last):
                at = (dx, m, y_rows(d), slice(None))
                ss[at] = (ss[at].astype(F32) + via[dx, m].astype(F32)).astype(BF16)
            at = pl.ds(first, last - first)
            sent += [to_owner(dx, part, at), to_owner(dx, part + 2, at)]
        return sent

    partial(0, 0, 2)
    started0 = launch(0, 0, 2)
    wf0.wait_recv()
    wf1.wait_recv()
    partial(0, 2, 4)
    started00 = launch(0, 2, 4)
    r0 = pass_on(0, 0, 2, started0) + pass_on(0, 2, 4, started00)
    forwards = []
    for part in range(2):
        c_pairs[part][0].wait_recv()
        a = send(ctx.at[3, part, pl.ds(0, 2)], ctx.at[2, part, pl.ds(0, 2)], x_by(1))
        c_pairs[part][1].wait_recv()
        b = send(ctx.at[1, part, pl.ds(2, 2)], ctx.at[2, part, pl.ds(2, 2)], x_by(-1))
        forwards += [a, b]
    partial(1, 0, 4)
    started1 = launch(1, 0, 4)
    partial(3, 0, 4)
    started3 = launch(3, 0, 4)
    r1 = pass_on(1, 0, 4, started1)
    for copy in forwards:
        copy.wait_recv()
    partial(2, 0, 4)
    started2 = launch(2, 0, 4)
    r3 = pass_on(3, 0, 4, started3)
    r2 = pass_on(2, 0, 4, started2)

    own_block = pl.ds(pl.multiple_of(group * 32, 32), 32)
    back = []
    for dx, sent in ((0, r0), (1, r1), (3, r3), (2, r2)):
        for copy in sent:
            copy.wait_recv()

        @pl.loop(0, 4)
        def _(m):
            total = ss[dx, m, own_block, :].astype(F32)
            for k in range(len(PLANE)):
                total += red[dx, k, m].astype(F32)
            if dx == 0:
                parts[m] = total.astype(BF16)
            else:
                fin[dx, m] = total.astype(BF16)
        if dx != 0:
            back.append(send(fin.at[dx], parts.at[pl.ds((4 - dx) % 4 * 4, 4)], x_by(dx)))
    for copy in back:
        copy.wait_recv()

    out[...] = parts[...]
    for copy in copies:
        copy.wait_send()


def place(held, parts, out):
    rep = lax.axis_index("rep")
    for r in range(16):
        slot = (r // 4 + 4 - rep // 4) % 4 * 4 + (r % 4 + 4 - rep % 4) % 4
        out[:, pl.ds(pl.multiple_of(held[r] * SL, SL), SL)] = parts[slot]


N_COPIES = 38 + 15 + 4 + 1 + 8 + 5 * 12 + 3


def tables():
    p = np.arange(SEQ)
    where_at = (p // 128 * 128 + p // 32 % 2 * 64 + p // 64 % 2 * 32 + p % 32).astype(np.float32)
    freqs = np.float32(ROPE_THETA) ** (-(np.arange(HD // 2, dtype=np.float32) * np.float32(2.0)) / np.float32(HD))
    angles = where_at[:, None] * freqs[None, :]
    cosine, sine = np.cos(angles), np.sin(angles)
    return (np.concatenate([cosine, cosine], 1).astype(np.float32),
            np.concatenate([-sine, sine], 1).astype(np.float32))


def per_device(hidden, norm_gain, q_weight, kv_weight, out_weight, held_slice):
    cosine, sine = tables()
    vm = pltpu.VMEM
    parts = pl.pallas_call(
        kernel,
        out_shape=jax.ShapeDtypeStruct((16, 32, SL), BF16),
        in_specs=[pl.BlockSpec(memory_space=pltpu.SMEM)] + [pl.BlockSpec(memory_space=pl.ANY)] * 7,
        out_specs=pl.BlockSpec(memory_space=pltpu.VMEM),
        scratch_shapes=[
            vm((32, D), BF16), vm((D // HD, HD), BF16), vm((SEQ, HD), F32), vm((SEQ, HD), F32),
            vm((16, SEQ, SL), BF16), vm((4, 4, SL, WC), BF16), vm((4, SL, SL), BF16), vm((SEQ, WC), F32),
            vm((2, SEQ, HD), BF16), vm((4, SEQ, HD), BF16), vm((4, 2, 4, 2, 64, 256), BF16),
            vm((4, 4, 256, SL), BF16), vm((4, 4, 256, SL), BF16), vm((4, 4, 256, SL), BF16),
            vm((4, 4, 64, SL), BF16), vm((4, 5, 4, 32, SL), BF16), vm((4, 4, 32, SL), BF16), vm((16, 32, SL), BF16),
            pltpu.SemaphoreType.DMA((7,)), pltpu.SemaphoreType.DMA((N_COPIES,)), pltpu.SemaphoreType.DMA((N_COPIES,)),
        ],
        compiler_params=pltpu.CompilerParams(
            collective_id=0, has_side_effects=True, vmem_limit_bytes=62 * 1024 * 1024),
        name="block",
    )(held_slice, hidden, norm_gain.reshape(D // HD, HD), q_weight, kv_weight, out_weight,
      jnp.asarray(cosine), jnp.asarray(sine))
    return pl.pallas_call(
        place,
        out_shape=jax.ShapeDtypeStruct((32, D), BF16),
        in_specs=[pl.BlockSpec(memory_space=pltpu.SMEM), pl.BlockSpec(memory_space=pltpu.VMEM)],
        out_specs=pl.BlockSpec(memory_space=pltpu.VMEM),
        name="place",
    )(held_slice, parts)


def solution(mesh):
    return jax.shard_map(
        per_device,
        mesh=mesh,
        in_specs=(P(("rep", "tp"), None), P(), P("rep", "tp"), P("rep", None), P("tp", "rep"), P()),
        out_specs=P(("rep", "tp"), None),
        check_vma=False,
    )
```

```python
import jax
import jax.numpy as jnp
import numpy as np
from jax import lax
from jax.experimental import pallas as pl
from jax.experimental.pallas import tpu as pltpu
from jax.sharding import PartitionSpec as P

HD = 128
HQ = 64
KVH = 8
D = 8192
SEQ = 512
SL = 512
WC = 640
ROPE_THETA = 500000.0
MESH = pl.DeviceIdType.MESH
F32, BF16 = jnp.float32, jnp.bfloat16

CORE = (0, 0, 0, 0, 1)
ZL = (0, 0, 0, 1, 0)
PLANE = [(0, 1, 0, 0, 0), (0, 3, 0, 0, 0), (0, 1, 0, 1, 0), (0, 3, 0, 1, 0), ZL]


def x_by(d):
    return (d % 4, 0, 0, 0, 0)


def z_by(d):
    return (0, 0, d % 4, 0, 0)


def y_by(d):
    return (0, d % 4, 0, 0, 0)


PEERS = [x_by(1), x_by(2), x_by(3), z_by(1), z_by(3), y_by(2), CORE] + PLANE


def kernel(held, hidden, gain, q_weight, kv_weight, out_weight, cos_hbm, sin_hbm, out,
           hid, gn, cos, sin, tok, w, wo, acc, kv, q, ctx, give, got, ss, via, red, fin, parts, lsem, ssem, rsem):
    rep, tp = lax.axis_index("rep"), lax.axis_index("tp")
    x, zh = rep // 4, rep % 4
    y, zl, c = tp // 4, (tp // 2) % 2, tp % 2

    def target(rel):
        dx, dy, dz, dl, dc = rel
        return (
            (x + dx) % 4 * 4 + (zh + dz) % 4,
            (y + dy) % 4 * 4 + (zl + dl) % 2 * 2 + (c + dc) % 2,
        )

    copies = []

    def send(src, dst, rel):
        k = len(copies)
        copy = pltpu.make_async_remote_copy(
            src_ref=src, dst_ref=dst, send_sem=ssem.at[k], recv_sem=rsem.at[k],
            device_id=target(rel), device_id_type=MESH)
        copy.start()
        copies.append(copy)
        return copy

    group = y * 2 + zl
    locals_ = [
        pltpu.make_async_copy(q_weight, w.at[0, :, pl.ds(0, SL)], lsem.at[0]),
        pltpu.make_async_copy(
            kv_weight.at[:, pl.ds(pl.multiple_of(c * KVH * HD + group * HD, HD), HD)],
            w.at[0, :, pl.ds(SL, HD)], lsem.at[1]),
        pltpu.make_async_copy(hidden, hid, lsem.at[2]),
        pltpu.make_async_copy(gain, gn, lsem.at[3]),
        pltpu.make_async_copy(out_weight, wo.at[0], lsem.at[4]),
        pltpu.make_async_copy(cos_hbm, cos, lsem.at[5]),
        pltpu.make_async_copy(sin_hbm, sin, lsem.at[6]),
    ]
    for copy in locals_:
        copy.start()

    barrier = pltpu.get_barrier_semaphore()
    for rel in PEERS:
        pl.semaphore_signal(barrier, inc=1, device_id=target(rel), device_id_type=MESH)
    pl.semaphore_wait(barrier, len(PEERS))

    def half(dx, dz, part):
        return w.at[dx % 4 * 4 + dz % 4, pl.ds(part * (SL // 2), SL // 2), :]

    def x_send(dz, part, d):
        return send(half(0, dz, part), half(-d, dz, part), x_by(d))

    def x_forward(copy, dz, part):
        copy.wait_recv()
        d = 1 - 2 * part
        return send(half(-d, dz, part), half(-2 * d, dz, part), x_by(d))

    locals_[0].wait()
    locals_[1].wait()
    z_first = send(half(0, 0, 0), half(0, -1, 0), z_by(1)), send(half(0, 0, 1), half(0, 1, 1), z_by(-1))
    xs = {}
    for part in range(2):
        xs[0, part, 1] = x_send(0, part, 1)
        xs[0, 1 - part, -1] = x_send(0, 1 - part, -1)

    z_second = send(half(0, 0, 1), half(0, -1, 1), z_by(1)), send(half(0, 0, 0), half(0, 1, 0), z_by(-1))

    def rows(dy, dl, dc=0):
        return pl.ds(pl.multiple_of((y + dy) % 4 * 128 + (c + dc) % 2 * 64 + (zl + dl) % 2 * 32, 32), 32)

    locals_[2].wait()
    locals_[3].wait()
    states = hid[...].astype(F32)
    factor = lax.rsqrt(jnp.mean(states * states, axis=-1, keepdims=True) + 1e-05)
    for n in range(D // HD):
        one = hid[:, n * HD:(n + 1) * HD].astype(F32) * factor * gn[n:n + 1, :].astype(F32)
        tok[n // 4, rows(0, 0), n % 4 * HD:(n % 4 + 1) * HD] = one.astype(BF16)

    def tok_at(dy, dl):
        return tok.at[:, rows(dy, dl), :]

    t_z = send(tok_at(0, 0), tok_at(0, 0), ZL)
    t_y0 = [send(tok_at(0, 0), tok_at(0, 0), y_by(d)) for d in (1, 3, 2)]
    t_core = [send(tok_at(0, 0), tok_at(0, 0), CORE)]

    ends = [(0, x_forward(xs[0, 0, 1], 0, 0), x_forward(xs[0, 1, -1], 0, 1))]
    z_first[0].wait_recv()
    zf0 = send(half(0, -1, 0), half(0, -2, 0), z_by(1))
    for d in (1, -1):
        xs[-1, 0, d] = x_send(-1, 0, d)
    z_first[1].wait_recv()
    zf1 = send(half(0, 1, 1), half(0, 2, 1), z_by(-1))
    for d in (-1, 1):
        xs[1, 1, d] = x_send(1, 1, d)
    z_second[0].wait_recv()
    for d in (-1, 1):
        xs[-1, 1, d] = x_send(-1, 1, d)
    z_second[1].wait_recv()
    for d in (1, -1):
        xs[1, 0, d] = x_send(1, 0, d)
    f30 = x_forward(xs[-1, 0, 1], -1, 0)
    f11 = x_forward(xs[1, 1, -1], 1, 1)
    for d, copy in zip((1, 3, 2), t_y0):
        copy.wait_recv()
        t_core.append(send(tok_at(-d, 0), tok_at(-d, 0), CORE))
    t_z.wait_recv()
    t_y1 = [send(tok_at(0, 1), tok_at(0, 1), y_by(d)) for d in (1, 3, 2)]
    t_core.append(send(tok_at(0, 1), tok_at(0, 1), CORE))
    locals_[4].wait()
    wo_pair = send(wo.at[0], wo.at[3], z_by(1)), send(wo.at[0], wo.at[1], z_by(-1))
    zf0.wait_recv()
    for d in (1, -1):
        xs[2, 0, d] = x_send(2, 0, d)
    zf1.wait_recv()
    for d in (-1, 1):
        xs[2, 1, d] = x_send(2, 1, d)
    ends.append((-1, f30, x_forward(xs[-1, 1, -1], -1, 1)))
    ends.append((1, x_forward(xs[1, 0, 1], 1, 0), f11))
    for d, copy in zip((1, 3, 2), t_y1):
        copy.wait_recv()
        t_core.append(send(tok_at(-d, 1), tok_at(-d, 1), CORE))
    for copy in t_core:
        copy.wait_recv()

    acc[...] = jnp.zeros_like(acc)

    def project(dx, dz):
        source = held[(x + dx) % 4 * 4 + (zh + dz) % 4]
        slot = dx % 4 * 4 + dz % 4

        @pl.loop(0, 2)
        def _(i):
            at = pl.ds(pl.multiple_of(i * 256, 256), 256)
            acc[at, :] += jnp.dot(tok[source, at, :], w[slot], preferred_element_type=F32)

    for dz in (0, -1, 1, 2):
        project(0, dz)
    for dz in (0, -1, 1):
        xs[dz, 1, 1].wait_recv()
        project(-1, dz)
        xs[dz, 0, -1].wait_recv()
        project(1, dz)
    ends.append((2, x_forward(xs[2, 0, 1], 2, 0), x_forward(xs[2, 1, -1], 2, 1)))
    wo_pair[0].wait_recv()
    wf0 = send(wo.at[3, pl.ds(0, 256), :], wo.at[2, pl.ds(0, 256), :], z_by(1))
    wo_pair[1].wait_recv()
    wf1 = send(wo.at[1, pl.ds(256, 256), :], wo.at[2, pl.ds(256, 256), :], z_by(-1))
    xs[2, 1, 1].wait_recv()
    project(-1, 2)
    xs[2, 0, -1].wait_recv()
    project(1, 2)
    for dz, a, b in ends:
        a.wait_recv()
        b.wait_recv()
        project(2, dz)

    locals_[5].wait()
    locals_[6].wait()
    pair_own = acc[:, SL:WC]
    turned = pair_own * cos[...] + pltpu.roll(pair_own, HD // 2, 1) * sin[...]
    kv[c] = jnp.where(c == 0, turned, pair_own).astype(BF16)
    kv_copy = send(kv.at[c], kv.at[c], CORE)
    for n in range(4):
        one = acc[:, n * HD:(n + 1) * HD]
        q[n] = (one * cos[...] + pltpu.roll(one, HD // 2, 1) * sin[...]).astype(BF16)
    kv_copy.wait_recv()

    def position(p):
        return p // 32 % 2 * 64 + p // 64 * 32 + p % 32

    earlier = (position(lax.broadcasted_iota(jnp.int32, (HD, 1), 0))
               >= position(lax.broadcasted_iota(jnp.int32, (1, HD), 1)))
    scale = HD**-0.5 / np.log(2.0)

    def heads(part):
        for n in range(2):
            for b in range(4):
                end = (b + 1) * 128
                scores = lax.dot_general(
                    q[part * 2 + n, b * 128:end, :], kv[0, :end, :], (((1,), (1,)), ((), ())),
                    preferred_element_type=F32)
                near = jnp.where(earlier, scores[:, end - 128:], -1e30)
                scores = jnp.concatenate([scores[:, :end - 128], near], axis=1) if b else near
                weights = jnp.exp2((scores - jnp.max(scores, axis=-1, keepdims=True)) * scale)
                probs = (weights * (1.0 / jnp.sum(weights, axis=-1, keepdims=True))).astype(BF16)
                mixed = jnp.dot(probs, kv[1, :end, :], preferred_element_type=F32).astype(BF16)
                ctx[0, part, b, :, :, n * HD:(n + 1) * HD] = mixed.reshape(2, 64, HD)

    c_pairs = []
    for part in range(2):
        heads(part)
        c_pairs.append((send(ctx.at[0, part], ctx.at[3, part], x_by(1)),
                        send(ctx.at[0, part], ctx.at[1, part], x_by(-1))))

    def product(dx, core, m):
        first, second = (ctx[dx, part, :, core].reshape(256, 256) for part in range(2))
        return (jnp.dot(first, wo[m, pl.ds(0, 256), :], preferred_element_type=F32)
                + jnp.dot(second, wo[m, pl.ds(256, 256), :], preferred_element_type=F32)).astype(BF16)

    def y_rows(d):
        return pl.ds(pl.multiple_of((y + d) % 4 * 64, 64), 64)

    def partial(dx, lo, hi):
        @pl.loop(lo, hi)
        def _(m):
            give[dx, m] = product(dx, 1 - c, m)
        at = pl.ds(lo, hi - lo)
        swap = send(give.at[dx, at], got.at[dx, at], CORE)

        @pl.loop(lo, hi)
        def _(m):
            ss[dx, m] = product(dx, c, m)
        swap.wait_recv()

        @pl.loop(lo, hi)
        def _(m):
            ss[dx, m] = (ss[dx, m].astype(F32) + got[dx, m].astype(F32)).astype(BF16)

    def to_owner(dx, k, at):
        rel = PLANE[k]
        block = pl.ds(pl.multiple_of((y + rel[1]) % 4 * 64 + (zl + rel[3]) % 2 * 32, 32), 32)
        return send(ss.at[dx, at, block, :], red.at[dx, k, at], rel)

    def launch(dx, lo, hi):
        mid = (lo + hi) // 2
        low, high = pl.ds(lo, mid - lo), pl.ds(mid, hi - mid)
        up = send(ss.at[dx, low, y_rows(2), :], via.at[dx, low], y_by(1))
        down = send(ss.at[dx, high, y_rows(2), :], via.at[dx, high], y_by(-1))
        sent = [to_owner(dx, 0, high), to_owner(dx, 1, low), to_owner(dx, 2, high), to_owner(dx, 3, low),
                to_owner(dx, 4, pl.ds(lo, hi - lo))]
        return up, down, sent

    def pass_on(dx, lo, hi, started):
        mid = (lo + hi) // 2
        sent = started[2]
        for part, d, first, last in ((0, 1, lo, mid), (1, 3, mid, hi)):
            started[part].wait_recv()
            for m in range(first, last):
                at = (dx, m, y_rows(d), slice(None))
                ss[at] = (ss[at].astype(F32) + via[dx, m].astype(F32)).astype(BF16)
            at = pl.ds(first, last - first)
            sent += [to_owner(dx, part, at), to_owner(dx, part + 2, at)]
        return sent

    partial(0, 0, 2)
    started0 = launch(0, 0, 2)
    wf0.wait_recv()
    wf1.wait_recv()
    partial(0, 2, 4)
    started00 = launch(0, 2, 4)
    r0 = pass_on(0, 0, 2, started0) + pass_on(0, 2, 4, started00)
    forwards = []
    for part in range(2):
        c_pairs[part][0].wait_recv()
        a = send(ctx.at[3, part, pl.ds(0, 2)], ctx.at[2, part, pl.ds(0, 2)], x_by(1))
        c_pairs[part][1].wait_recv()
        b = send(ctx.at[1, part, pl.ds(2, 2)], ctx.at[2, part, pl.ds(2, 2)], x_by(-1))
        forwards += [a, b]
    partial(1, 0, 4)
    started1 = launch(1, 0, 4)
    partial(3, 0, 4)
    started3 = launch(3, 0, 4)
    r1 = pass_on(1, 0, 4, started1)
    for copy in forwards:
        copy.wait_recv()
    partial(2, 0, 4)
    started2 = launch(2, 0, 4)
    r3 = pass_on(3, 0, 4, started3)
    r2 = pass_on(2, 0, 4, started2)

    own_block = pl.ds(pl.multiple_of(group * 32, 32), 32)
    back = []
    for dx, sent in ((0, r0), (1, r1), (3, r3), (2, r2)):
        for copy in sent:
            copy.wait_recv()

        @pl.loop(0, 4)
        def _(m):
            total = ss[dx, m, own_block, :].astype(F32)
            for k in range(len(PLANE)):
                total += red[dx, k, m].astype(F32)
            if dx == 0:
                parts[m] = total.astype(BF16)
            else:
                fin[dx, m] = total.astype(BF16)
        if dx != 0:
            back.append(send(fin.at[dx], parts.at[pl.ds((4 - dx) % 4 * 4, 4)], x_by(dx)))
    for copy in back:
        copy.wait_recv()

    out[...] = parts[...]
    for copy in copies:
        copy.wait_send()


def place(held, parts, out):
    rep = lax.axis_index("rep")
    for r in range(16):
        slot = (r // 4 + 4 - rep // 4) % 4 * 4 + (r % 4 + 4 - rep % 4) % 4
        out[:, pl.ds(pl.multiple_of(held[r] * SL, SL), SL)] = parts[slot]


N_COPIES = 30 + 15 + 4 + 1 + 8 + 5 * 12 + 3


def tables():
    p = np.arange(SEQ)
    where_at = (p // 128 * 128 + p // 32 % 2 * 64 + p // 64 % 2 * 32 + p % 32).astype(np.float32)
    freqs = np.float32(ROPE_THETA) ** (-(np.arange(HD // 2, dtype=np.float32) * np.float32(2.0)) / np.float32(HD))
    angles = where_at[:, None] * freqs[None, :]
    cosine, sine = np.cos(angles), np.sin(angles)
    return (np.concatenate([cosine, cosine], 1).astype(np.float32),
            np.concatenate([-sine, sine], 1).astype(np.float32))


def per_device(hidden, norm_gain, q_weight, kv_weight, out_weight, held_slice):
    cosine, sine = tables()
    vm = pltpu.VMEM
    parts = pl.pallas_call(
        kernel,
        out_shape=jax.ShapeDtypeStruct((16, 32, SL), BF16),
        in_specs=[pl.BlockSpec(memory_space=pltpu.SMEM)] + [pl.BlockSpec(memory_space=pl.ANY)] * 7,
        out_specs=pl.BlockSpec(memory_space=pltpu.VMEM),
        scratch_shapes=[
            vm((32, D), BF16), vm((D // HD, HD), BF16), vm((SEQ, HD), F32), vm((SEQ, HD), F32),
            vm((16, SEQ, SL), BF16), vm((16, SL, WC), BF16), vm((4, SL, SL), BF16), vm((SEQ, WC), F32),
            vm((2, SEQ, HD), BF16), vm((4, SEQ, HD), BF16), vm((4, 2, 4, 2, 64, 256), BF16),
            vm((4, 4, 256, SL), BF16), vm((4, 4, 256, SL), BF16), vm((4, 4, 256, SL), BF16),
            vm((4, 4, 64, SL), BF16), vm((4, 5, 4, 32, SL), BF16), vm((4, 4, 32, SL), BF16), vm((16, 32, SL), BF16),
            pltpu.SemaphoreType.DMA((7,)), pltpu.SemaphoreType.DMA((N_COPIES,)), pltpu.SemaphoreType.DMA((N_COPIES,)),
        ],
        compiler_params=pltpu.CompilerParams(
            collective_id=0, has_side_effects=True, vmem_limit_bytes=62 * 1024 * 1024),
        name="block",
    )(held_slice, hidden, norm_gain.reshape(D // HD, HD), q_weight, kv_weight, out_weight,
      jnp.asarray(cosine), jnp.asarray(sine))
    return pl.pallas_call(
        place,
        out_shape=jax.ShapeDtypeStruct((32, D), BF16),
        in_specs=[pl.BlockSpec(memory_space=pltpu.SMEM), pl.BlockSpec(memory_space=pltpu.VMEM)],
        out_specs=pl.BlockSpec(memory_space=pltpu.VMEM),
        name="place",
    )(held_slice, parts)


def solution(mesh):
    return jax.shard_map(
        per_device,
        mesh=mesh,
        in_specs=(P(("rep", "tp"), None), P(), P("rep", "tp"), P("rep", None), P("tp", "rep"), P()),
        out_specs=P(("rep", "tp"), None),
        check_vma=False,
    )
```

```python
import jax
import jax.numpy as jnp
import numpy as np
from jax import lax
from jax.experimental import pallas as pl
from jax.experimental.pallas import tpu as pltpu
from jax.sharding import PartitionSpec as P

HD = 128
HQ = 64
KVH = 8
D = 8192
SEQ = 512
SL = 512
WC = 640
ROPE_THETA = 500000.0
MESH = pl.DeviceIdType.MESH
F32, BF16 = jnp.float32, jnp.bfloat16

CORE = (0, 0, 0, 0, 1)
ZL = (0, 0, 0, 1, 0)
PLANE = [(0, 1, 0, 0, 0), (0, 3, 0, 0, 0), (0, 1, 0, 1, 0), (0, 3, 0, 1, 0), ZL]


def x_by(d):
    return (d % 4, 0, 0, 0, 0)


def z_by(d):
    return (0, 0, d % 4, 0, 0)


def y_by(d):
    return (0, d % 4, 0, 0, 0)


PEERS = [x_by(1), x_by(2), x_by(3), z_by(1), z_by(3), y_by(2), CORE] + PLANE


def kernel(held, hidden, gain, q_weight, kv_weight, out_weight, cos_hbm, sin_hbm, out,
           hid, gn, cos, sin, tok, w, wo, acc, kv, q, ctx, give, got, ss, via, red, fin, parts, lsem, ssem, rsem):
    rep, tp = lax.axis_index("rep"), lax.axis_index("tp")
    x, zh = rep // 4, rep % 4
    y, zl, c = tp // 4, (tp // 2) % 2, tp % 2

    def target(rel):
        dx, dy, dz, dl, dc = rel
        return (
            (x + dx) % 4 * 4 + (zh + dz) % 4,
            (y + dy) % 4 * 4 + (zl + dl) % 2 * 2 + (c + dc) % 2,
        )

    copies = []

    def send(src, dst, rel):
        k = len(copies)
        copy = pltpu.make_async_remote_copy(
            src_ref=src, dst_ref=dst, send_sem=ssem.at[k], recv_sem=rsem.at[k],
            device_id=target(rel), device_id_type=MESH)
        copy.start()
        copies.append(copy)
        return copy

    group = y * 2 + zl
    locals_ = [
        pltpu.make_async_copy(q_weight, w.at[0, :, pl.ds(0, SL)], lsem.at[0]),
        pltpu.make_async_copy(
            kv_weight.at[:, pl.ds(pl.multiple_of(c * KVH * HD + group * HD, HD), HD)],
            w.at[0, :, pl.ds(SL, HD)], lsem.at[1]),
        pltpu.make_async_copy(hidden, hid, lsem.at[2]),
        pltpu.make_async_copy(gain, gn, lsem.at[3]),
        pltpu.make_async_copy(out_weight, wo.at[0], lsem.at[4]),
        pltpu.make_async_copy(cos_hbm, cos, lsem.at[5]),
        pltpu.make_async_copy(sin_hbm, sin, lsem.at[6]),
    ]
    for copy in locals_:
        copy.start()

    barrier = pltpu.get_barrier_semaphore()
    for rel in PEERS:
        pl.semaphore_signal(barrier, inc=1, device_id=target(rel), device_id_type=MESH)
    pl.semaphore_wait(barrier, len(PEERS))

    def half(dx, dz, part):
        return w.at[dx % 4 * 4 + dz % 4, pl.ds(part * (SL // 2), SL // 2), :]

    def x_send(dz, part, d):
        return send(half(0, dz, part), half(-d, dz, part), x_by(d))

    def x_forward(copy, dz, part):
        copy.wait_recv()
        d = 1 - 2 * part
        return send(half(-d, dz, part), half(-2 * d, dz, part), x_by(d))

    locals_[0].wait()
    locals_[1].wait()
    z_first = send(half(0, 0, 0), half(0, -1, 0), z_by(1)), send(half(0, 0, 1), half(0, 1, 1), z_by(-1))
    xs = {}
    for part in range(2):
        xs[0, part, 1] = x_send(0, part, 1)
        xs[0, 1 - part, -1] = x_send(0, 1 - part, -1)

    z_second = send(half(0, 0, 1), half(0, -1, 1), z_by(1)), send(half(0, 0, 0), half(0, 1, 0), z_by(-1))

    def rows(dy, dl, dc=0):
        return pl.ds(pl.multiple_of((y + dy) % 4 * 128 + (c + dc) % 2 * 64 + (zl + dl) % 2 * 32, 32), 32)

    locals_[2].wait()
    locals_[3].wait()
    states = hid[...].astype(F32)
    factor = lax.rsqrt(jnp.mean(states * states, axis=-1, keepdims=True) + 1e-05)
    for n in range(D // HD):
        one = hid[:, n * HD:(n + 1) * HD].astype(F32) * factor * gn[n:n + 1, :].astype(F32)
        tok[n // 4, rows(0, 0), n % 4 * HD:(n % 4 + 1) * HD] = one.astype(BF16)

    def tok_at(dy, dl):
        return tok.at[:, rows(dy, dl), :]

    t_z = send(tok_at(0, 0), tok_at(0, 0), ZL)
    t_y0 = [send(tok_at(0, 0), tok_at(0, 0), y_by(d)) for d in (1, 3, 2)]
    t_core = [send(tok_at(0, 0), tok_at(0, 0), CORE)]

    ends = [(0, x_forward(xs[0, 0, 1], 0, 0), x_forward(xs[0, 1, -1], 0, 1))]
    z_first[0].wait_recv()
    zf0 = send(half(0, -1, 0), half(0, -2, 0), z_by(1))
    for d in (1, -1):
        xs[-1, 0, d] = x_send(-1, 0, d)
    z_first[1].wait_recv()
    zf1 = send(half(0, 1, 1), half(0, 2, 1), z_by(-1))
    for d in (-1, 1):
        xs[1, 1, d] = x_send(1, 1, d)
    z_second[0].wait_recv()
    for d in (-1, 1):
        xs[-1, 1, d] = x_send(-1, 1, d)
    z_second[1].wait_recv()
    for d in (1, -1):
        xs[1, 0, d] = x_send(1, 0, d)
    f30 = x_forward(xs[-1, 0, 1], -1, 0)
    f11 = x_forward(xs[1, 1, -1], 1, 1)
    for d, copy in zip((1, 3, 2), t_y0):
        copy.wait_recv()
        t_core.append(send(tok_at(-d, 0), tok_at(-d, 0), CORE))
    t_z.wait_recv()
    t_y1 = [send(tok_at(0, 1), tok_at(0, 1), y_by(d)) for d in (1, 3, 2)]
    t_core.append(send(tok_at(0, 1), tok_at(0, 1), CORE))
    locals_[4].wait()
    wo_pair = send(wo.at[0], wo.at[3], z_by(1)), send(wo.at[0], wo.at[1], z_by(-1))
    zf0.wait_recv()
    for d in (1, -1):
        xs[2, 0, d] = x_send(2, 0, d)
    zf1.wait_recv()
    for d in (-1, 1):
        xs[2, 1, d] = x_send(2, 1, d)
    ends.append((-1, f30, x_forward(xs[-1, 1, -1], -1, 1)))
    ends.append((1, x_forward(xs[1, 0, 1], 1, 0), f11))
    for d, copy in zip((1, 3, 2), t_y1):
        copy.wait_recv()
        t_core.append(send(tok_at(-d, 1), tok_at(-d, 1), CORE))
    ends.append((2, x_forward(xs[2, 0, 1], 2, 0), x_forward(xs[2, 1, -1], 2, 1)))
    for copy in t_core:
        copy.wait_recv()

    acc[...] = jnp.zeros_like(acc)

    def project(dx, dz):
        source = held[(x + dx) % 4 * 4 + (zh + dz) % 4]
        slot = dx % 4 * 4 + dz % 4

        @pl.loop(0, 2)
        def _(i):
            at = pl.ds(pl.multiple_of(i * 256, 256), 256)
            acc[at, :] += jnp.dot(tok[source, at, :], w[slot], preferred_element_type=F32)

    for dz in (0, -1, 1, 2):
        project(0, dz)
    for dz in (0, -1, 1):
        xs[dz, 1, 1].wait_recv()
        project(-1, dz)
        xs[dz, 0, -1].wait_recv()
        project(1, dz)
    for dz, a, b in ends[:3]:
        a.wait_recv()
        b.wait_recv()
        project(2, dz)
    wo_pair[0].wait_recv()
    wf0 = send(wo.at[3, pl.ds(0, 256), :], wo.at[2, pl.ds(0, 256), :], z_by(1))
    wo_pair[1].wait_recv()
    wf1 = send(wo.at[1, pl.ds(256, 256), :], wo.at[2, pl.ds(256, 256), :], z_by(-1))
    xs[2, 1, 1].wait_recv()
    project(-1, 2)
    xs[2, 0, -1].wait_recv()
    project(1, 2)
    ends[3][1].wait_recv()
    ends[3][2].wait_recv()
    project(2, 2)

    locals_[5].wait()
    locals_[6].wait()
    pair_own = acc[:, SL:WC]
    turned = pair_own * cos[...] + pltpu.roll(pair_own, HD // 2, 1) * sin[...]
    kv[c] = jnp.where(c == 0, turned, pair_own).astype(BF16)
    kv_copy = send(kv.at[c], kv.at[c], CORE)
    for n in range(4):
        one = acc[:, n * HD:(n + 1) * HD]
        q[n] = (one * cos[...] + pltpu.roll(one, HD // 2, 1) * sin[...]).astype(BF16)
    kv_copy.wait_recv()

    def position(p):
        return p // 32 % 2 * 64 + p // 64 * 32 + p % 32

    earlier = (position(lax.broadcasted_iota(jnp.int32, (HD, 1), 0))
               >= position(lax.broadcasted_iota(jnp.int32, (1, HD), 1)))
    scale = HD**-0.5 / np.log(2.0)

    def heads(part):
        for n in range(2):
            for b in range(4):
                end = (b + 1) * 128
                scores = lax.dot_general(
                    q[part * 2 + n, b * 128:end, :], kv[0, :end, :], (((1,), (1,)), ((), ())),
                    preferred_element_type=F32)
                near = jnp.where(earlier, scores[:, end - 128:], -1e30)
                scores = jnp.concatenate([scores[:, :end - 128], near], axis=1) if b else near
                weights = jnp.exp2((scores - jnp.max(scores, axis=-1, keepdims=True)) * scale)
                probs = (weights * (1.0 / jnp.sum(weights, axis=-1, keepdims=True))).astype(BF16)
                mixed = jnp.dot(probs, kv[1, :end, :], preferred_element_type=F32).astype(BF16)
                ctx[0, part, b, :, :, n * HD:(n + 1) * HD] = mixed.reshape(2, 64, HD)

    c_pairs = []
    for part in range(2):
        heads(part)
        c_pairs.append((send(ctx.at[0, part], ctx.at[3, part], x_by(1)),
                        send(ctx.at[0, part], ctx.at[1, part], x_by(-1))))

    def product(dx, core, m):
        first, second = (ctx[dx, part, :, core].reshape(256, 256) for part in range(2))
        return (jnp.dot(first, wo[m, pl.ds(0, 256), :], preferred_element_type=F32)
                + jnp.dot(second, wo[m, pl.ds(256, 256), :], preferred_element_type=F32)).astype(BF16)

    def y_rows(d):
        return pl.ds(pl.multiple_of((y + d) % 4 * 64, 64), 64)

    def partial(dx, lo, hi):
        @pl.loop(lo, hi)
        def _(m):
            give[dx, m] = product(dx, 1 - c, m)
        at = pl.ds(lo, hi - lo)
        swap = send(give.at[dx, at], got.at[dx, at], CORE)

        @pl.loop(lo, hi)
        def _(m):
            ss[dx, m] = product(dx, c, m)
        swap.wait_recv()

        @pl.loop(lo, hi)
        def _(m):
            ss[dx, m] = (ss[dx, m].astype(F32) + got[dx, m].astype(F32)).astype(BF16)

    def to_owner(dx, k, at):
        rel = PLANE[k]
        block = pl.ds(pl.multiple_of((y + rel[1]) % 4 * 64 + (zl + rel[3]) % 2 * 32, 32), 32)
        return send(ss.at[dx, at, block, :], red.at[dx, k, at], rel)

    def launch(dx, lo, hi):
        mid = (lo + hi) // 2
        low, high = pl.ds(lo, mid - lo), pl.ds(mid, hi - mid)
        up = send(ss.at[dx, low, y_rows(2), :], via.at[dx, low], y_by(1))
        down = send(ss.at[dx, high, y_rows(2), :], via.at[dx, high], y_by(-1))
        sent = [to_owner(dx, 0, high), to_owner(dx, 1, low), to_owner(dx, 2, high), to_owner(dx, 3, low),
                to_owner(dx, 4, pl.ds(lo, hi - lo))]
        return up, down, sent

    def pass_on(dx, lo, hi, started):
        mid = (lo + hi) // 2
        sent = started[2]
        for part, d, first, last in ((0, 1, lo, mid), (1, 3, mid, hi)):
            started[part].wait_recv()
            for m in range(first, last):
                at = (dx, m, y_rows(d), slice(None))
                ss[at] = (ss[at].astype(F32) + via[dx, m].astype(F32)).astype(BF16)
            at = pl.ds(first, last - first)
            sent += [to_owner(dx, part, at), to_owner(dx, part + 2, at)]
        return sent

    partial(0, 0, 2)
    started0 = launch(0, 0, 2)
    wf0.wait_recv()
    wf1.wait_recv()
    partial(0, 2, 4)
    started00 = launch(0, 2, 4)
    r0 = pass_on(0, 0, 2, started0) + pass_on(0, 2, 4, started00)
    forwards = []
    for part in range(2):
        c_pairs[part][0].wait_recv()
        a = send(ctx.at[3, part, pl.ds(0, 2)], ctx.at[2, part, pl.ds(0, 2)], x_by(1))
        c_pairs[part][1].wait_recv()
        b = send(ctx.at[1, part, pl.ds(2, 2)], ctx.at[2, part, pl.ds(2, 2)], x_by(-1))
        forwards += [a, b]
    partial(1, 0, 4)
    started1 = launch(1, 0, 4)
    partial(3, 0, 4)
    started3 = launch(3, 0, 4)
    r1 = pass_on(1, 0, 4, started1)
    for copy in forwards:
        copy.wait_recv()
    partial(2, 0, 4)
    started2 = launch(2, 0, 4)
    r3 = pass_on(3, 0, 4, started3)
    r2 = pass_on(2, 0, 4, started2)

    own_block = pl.ds(pl.multiple_of(group * 32, 32), 32)
    back = []
    for dx, sent in ((0, r0), (1, r1), (3, r3), (2, r2)):
        for copy in sent:
            copy.wait_recv()

        @pl.loop(0, 4)
        def _(m):
            total = ss[dx, m, own_block, :].astype(F32)
            for k in range(len(PLANE)):
                total += red[dx, k, m].astype(F32)
            if dx == 0:
                parts[m] = total.astype(BF16)
            else:
                fin[dx, m] = total.astype(BF16)
        if dx != 0:
            back.append(send(fin.at[dx], parts.at[pl.ds((4 - dx) % 4 * 4, 4)], x_by(dx)))
    for copy in back:
        copy.wait_recv()

    out[...] = parts[...]
    for copy in copies:
        copy.wait_send()


def place(held, parts, out):
    rep = lax.axis_index("rep")
    for r in range(16):
        slot = (r // 4 + 4 - rep // 4) % 4 * 4 + (r % 4 + 4 - rep % 4) % 4
        out[:, pl.ds(pl.multiple_of(held[r] * SL, SL), SL)] = parts[slot]


N_COPIES = 30 + 15 + 4 + 1 + 8 + 5 * 12 + 3


def tables():
    p = np.arange(SEQ)
    where_at = (p // 128 * 128 + p // 32 % 2 * 64 + p // 64 % 2 * 32 + p % 32).astype(np.float32)
    freqs = np.float32(ROPE_THETA) ** (-(np.arange(HD // 2, dtype=np.float32) * np.float32(2.0)) / np.float32(HD))
    angles = where_at[:, None] * freqs[None, :]
    cosine, sine = np.cos(angles), np.sin(angles)
    return (np.concatenate([cosine, cosine], 1).astype(np.float32),
            np.concatenate([-sine, sine], 1).astype(np.float32))


def per_device(hidden, norm_gain, q_weight, kv_weight, out_weight, held_slice):
    cosine, sine = tables()
    vm = pltpu.VMEM
    parts = pl.pallas_call(
        kernel,
        out_shape=jax.ShapeDtypeStruct((16, 32, SL), BF16),
        in_specs=[pl.BlockSpec(memory_space=pltpu.SMEM)] + [pl.BlockSpec(memory_space=pl.ANY)] * 7,
        out_specs=pl.BlockSpec(memory_space=pltpu.VMEM),
        scratch_shapes=[
            vm((32, D), BF16), vm((D // HD, HD), BF16), vm((SEQ, HD), F32), vm((SEQ, HD), F32),
            vm((16, SEQ, SL), BF16), vm((16, SL, WC), BF16), vm((4, SL, SL), BF16), vm((SEQ, WC), F32),
            vm((2, SEQ, HD), BF16), vm((4, SEQ, HD), BF16), vm((4, 2, 4, 2, 64, 256), BF16),
            vm((4, 4, 256, SL), BF16), vm((4, 4, 256, SL), BF16), vm((4, 4, 256, SL), BF16),
            vm((4, 4, 64, SL), BF16), vm((4, 5, 4, 32, SL), BF16), vm((4, 4, 32, SL), BF16), vm((16, 32, SL), BF16),
            pltpu.SemaphoreType.DMA((7,)), pltpu.SemaphoreType.DMA((N_COPIES,)), pltpu.SemaphoreType.DMA((N_COPIES,)),
        ],
        compiler_params=pltpu.CompilerParams(
            collective_id=0, has_side_effects=True, vmem_limit_bytes=62 * 1024 * 1024),
        name="block",
    )(held_slice, hidden, norm_gain.reshape(D // HD, HD), q_weight, kv_weight, out_weight,
      jnp.asarray(cosine), jnp.asarray(sine))
    return pl.pallas_call(
        place,
        out_shape=jax.ShapeDtypeStruct((32, D), BF16),
        in_specs=[pl.BlockSpec(memory_space=pltpu.SMEM), pl.BlockSpec(memory_space=pltpu.VMEM)],
        out_specs=pl.BlockSpec(memory_space=pltpu.VMEM),
        name="place",
    )(held_slice, parts)


def solution(mesh):
    return jax.shard_map(
        per_device,
        mesh=mesh,
        in_specs=(P(("rep", "tp"), None), P(), P("rep", "tp"), P("rep", None), P("tp", "rep"), P()),
        out_specs=P(("rep", "tp"), None),
        check_vma=False,
    )
```
